32 devices in a mesh: lon: 8 (over z, y), lat: 4 (over x, core).
Axes of the slice: x: 2, y: 2, z: 4, core: 2. Of those that a mesh axis runs over, the one named last changes fastest.
Arguments:
- sample_deviations: float32 [32, 32, 32, 1024], P(None, None, 'lat', 'lon'), may hold values from -6 to 6
- east_courant: float32 [32, 32, 1024], P(None, 'lat', 'lon'), may hold values from -0.45 to 0.45
- north_courant: float32 [32, 32, 1024], P(None, 'lat', 'lon'), may hold values from -0.45 to 0.45
- production: float32 [32, 32, 1024], P(None, 'lat', 'lon'), may hold values from -1.8 to 1.8
- loss_rate: float32 [32, 32, 1024], P(None, 'lat', 'lon'), may hold values from 0.02 to 0.3
- entry_count: int32 [32], P(('lon', 'lat')), may hold values from 24 to 48, as said below
- entry_row: int32 [1536], P(('lon', 'lat')), may hold values from 0 to 7
- entry_block: int32 [1536], P(('lon', 'lat')), may hold values from 0 to 15
- path_weight: bfloat16 [1536, 128, 128], P(('lon', 'lat')), may hold values from 0 to 0.15234375
- observed: float32 [16384], P(('lon', 'lat')), may hold values from -288 to 288
- obs_var: float32 [16384], P(('lon', 'lat')), may hold values from 64 to 4608, as said below
Outputs:
- updated_samples: float32 [32, 32, 32, 1024], P(None, None, 'lat', 'lon')
- prior_samples_in_path_space: float32 [32, 16384], P(None, ('lon', 'lat'))
- scaled_innovation: float32 [16384], P(('lon', 'lat'))
The draws below stay inside these ranges and needn't reach their ends.
Inputs may be any that keep to these rules, and one draw needn't show every extreme that they name: `entry_count`: live crossing slots of each tile; some tile has all 48 live in every draw. `obs_var`: positive.
All inputs are finite; a program needn't handle non-finite values.
Results may differ from the reference program's by a relative error of at most 0.0025.
Values sent between devices are 32-bit elements; how exact they have to be, the bound alone decides.
No kernel may reach another device: no remote copies, remote signals or barrier semaphores. Data moves between devices by JAX's collectives and lax.ppermute only.
A program may use at most 64 MiB of HBM per device.

```python
import math
import jax
import jax.numpy as jnp
from jax import lax

SAMPLE_TOTAL = 32
ALTITUDE_LAYERS = 32
TILE_LAT = 8
TILE_LON = 128
RAY_BLOCK = 128
BLOCKS_DEV = 4
SLOTS_TILE = 48
GRID_LAT = 32
GRID_LON = 1024
COL_BLOCKS = 16
TILES = 32
RAYS = 16384
SLOTS = 1536


def draw_entry_count(key, part):
    tiles_lat = GRID_LAT // TILE_LAT
    tile_ids = jnp.arange(TILES)
    lat_pos = tile_ids % tiles_lat
    lower = SLOTS_TILE // 2
    upper = SLOTS_TILE + 1
    random_counts = jax.random.randint(key, (TILES,), lower, upper)
    return jnp.where(lat_pos == tiles_lat // 2, SLOTS_TILE, random_counts).astype(jnp.int32)


def draw_obs_var(key, part):
    per_tile = BLOCKS_DEV * RAY_BLOCK
    ray_ids = jnp.arange(RAYS)
    position = (ray_ids // per_tile).astype(jnp.float32) / max(TILES - 1, 1)
    baseline = RAYS / 256.0 * jnp.power(3.0, position)
    spread_factor = jnp.exp(jax.random.uniform(key, (RAYS,), jnp.float32, 0.0, math.log(8.0)))
    return (baseline * spread_factor).astype(jnp.float32)


def touch_ends(values, own_key, least, largest):
    extent = values.shape
    place = [jax.random.randint(jax.random.fold_in(own_key, axis), (), 0, extent[axis]) for axis in range(len(extent))]
    values = values.at[tuple(place)].set(least)
    longest = extent.index(max(extent))
    place[longest] = (place[longest] + 1) % extent[longest]
    return values.at[tuple(place)].set(largest)


def shard_levels(stream_key, extent, split, least, high):
    def one(dim, parts):
        heights = jax.random.uniform(jax.random.fold_in(jax.random.fold_in(stream_key, 6), dim), (parts,), jnp.float32, least / len(split), high / len(split))
        return jnp.repeat(jnp.exp(heights), extent[dim] // parts).reshape((-1,) + (1,) * (len(extent) - dim - 1))

    loudness = one(*split[0])
    for cut in split[1:]:
        loudness = loudness * one(*cut)
    return loudness


def normal_values(key, extent, width, reach, pieces=(), held_as=jnp.bfloat16):
    result = jax.random.normal(key, extent, jnp.float32) * width
    if len(pieces) > 0:
        result = shard_levels(key, extent, pieces, -0.22, 0.18) * result
    return jnp.clip(result, min=-reach, max=reach).astype(held_as)


def setup_inputs(seed: int = 0) -> dict:
    streams_of = jax.random.split(jax.random.key(seed), 12)
    sample_deviations = normal_values(streams_of[0], (SAMPLE_TOTAL, ALTITUDE_LAYERS, GRID_LAT, GRID_LON), 1.0, 6.0, ((2, 4), (3, 8)), jnp.float32)
    east_courant = jnp.clip(jax.random.uniform(streams_of[1], (ALTITUDE_LAYERS, GRID_LAT, GRID_LON), jnp.float32, -0.45, 0.45) * shard_levels(streams_of[1], (ALTITUDE_LAYERS, GRID_LAT, GRID_LON), ((1, 4), (2, 8)), -0.4, 0.0), -0.45, 0.45)
    north_courant = jnp.clip(jax.random.uniform(streams_of[2], (ALTITUDE_LAYERS, GRID_LAT, GRID_LON), jnp.float32, -0.45, 0.45) * shard_levels(streams_of[2], (ALTITUDE_LAYERS, GRID_LAT, GRID_LON), ((1, 4), (2, 8)), -0.4, 0.0), -0.45, 0.45)
    production = normal_values(streams_of[3], (ALTITUDE_LAYERS, GRID_LAT, GRID_LON), 0.3, 1.8, ((1, 4), (2, 8)), jnp.float32)
    loss_rate = jnp.clip(jnp.exp(math.log(0.3) - 2.7080503 * jax.random.uniform(streams_of[4], (ALTITUDE_LAYERS, GRID_LAT, GRID_LON), jnp.float32) ** shard_levels(streams_of[4], (ALTITUDE_LAYERS, GRID_LAT, GRID_LON), ((1, 4), (2, 8)), -0.2, 0.2)), 0.02, 0.3)
    entry_count = draw_entry_count(jax.random.fold_in(streams_of[11], 71), 0)
    entry_row = touch_ends(jax.random.randint(streams_of[6], (SLOTS,), 0, TILE_LAT), jax.random.fold_in(streams_of[6], 1), 0, TILE_LAT - 1).astype(jnp.int32)
    entry_block = touch_ends(jax.random.randint(streams_of[7], (SLOTS,), 0, COL_BLOCKS), jax.random.fold_in(streams_of[7], 1), 0, COL_BLOCKS - 1).astype(jnp.int32)
    path_weight = jnp.clip(0.15234375 * jax.random.uniform(streams_of[8], (SLOTS, TILE_LON, RAY_BLOCK), jnp.float32) ** shard_levels(streams_of[8], (SLOTS, TILE_LON, RAY_BLOCK), ((0, 32),), -0.2, 0.2), 0.0, 0.15234375).astype(jnp.bfloat16)
    observed = normal_values(streams_of[9], (RAYS,), 48.0, 288.0, ((0, 32),), jnp.float32)
    obs_var = draw_obs_var(jax.random.fold_in(streams_of[11], 71), 0)
    return dict(sample_deviations=sample_deviations, east_courant=east_courant, north_courant=north_courant, production=production, loss_rate=loss_rate, entry_count=entry_count, entry_row=entry_row, entry_block=entry_block, path_weight=path_weight, observed=observed, obs_var=obs_var)


highest = lax.Precision.HIGHEST

def advance(plasma_concentration, east_speed, north_speed, source, loss_rate):
    west_cell = jnp.roll(plasma_concentration, 1, axis=2)
    east_cell = jnp.roll(plasma_concentration, -1, axis=2)
    padded = jnp.pad(plasma_concentration, ((0, 0), (1, 1), (0, 0)))
    south_cell = padded[:, :-2, :]
    north_cell = padded[:, 2:, :]
    advected = plasma_concentration - jnp.maximum(east_speed, 0.0) * (plasma_concentration - west_cell) - jnp.minimum(east_speed, 0.0) * (east_cell - plasma_concentration)
    advected = advected - jnp.maximum(north_speed, 0.0) * (plasma_concentration - south_cell) - jnp.minimum(north_speed, 0.0) * (north_cell - plasma_concentration)
    return (1.0 - loss_rate) * advected + source

def analysis_weights(gram_sum, pull_sum):
    member_total = gram_sum.shape[0]
    identity = jnp.eye(member_total, dtype=gram_sum.dtype)
    factor_low = jnp.linalg.cholesky(gram_sum + (member_total - 1.0) * identity)
    halfway = lax.linalg.triangular_solve(factor_low, pull_sum[:, None], left_side=True, lower=True)
    mean_weights = lax.linalg.triangular_solve(factor_low, halfway, left_side=True, lower=True, transpose_a=True)
    inverse = lax.linalg.triangular_solve(factor_low, identity, left_side=True, lower=True)
    return mean_weights + math.sqrt(member_total - 1.0) * inverse.T

def reference(sample_deviations, east_courant, north_courant, production, loss_rate, entry_count, entry_row, entry_block, path_weight, observed, obs_var):

    def prior_sample(plasma_concentration):
        first_pass = advance(plasma_concentration, east_courant, north_courant, production, loss_rate)
        return advance(first_pass, east_courant, north_courant, production, loss_rate)
    prior_sample_set = lax.map(prior_sample, sample_deviations)
    column_integral_total = (lax.optimization_barrier(jnp.sum(prior_sample_set, axis=1)) / math.sqrt(ALTITUDE_LAYERS)).astype(jnp.bfloat16)
    tiles_lat = GRID_LAT // TILE_LAT
    rays_column = COL_BLOCKS * RAY_BLOCK
    slot_ids = jnp.arange(SLOTS_TILE, dtype=jnp.int32)
    block_ids = jnp.arange(COL_BLOCKS, dtype=jnp.int32)

    def tile_step(ray_total, tile_index):
        lon_pos = tile_index // tiles_lat
        lat_pos = tile_index % tiles_lat
        tile_patch = lax.dynamic_slice(column_integral_total, (jnp.int32(0), (lat_pos * TILE_LAT).astype(jnp.int32), (lon_pos * TILE_LON).astype(jnp.int32)), (SAMPLE_TOTAL, TILE_LAT, TILE_LON))
        slot_start = (tile_index * SLOTS_TILE).astype(jnp.int32)
        slot_rows = lax.dynamic_slice_in_dim(entry_row, slot_start, SLOTS_TILE)
        slot_blocks = lax.dynamic_slice_in_dim(entry_block, slot_start, SLOTS_TILE)
        slot_weights = lax.dynamic_slice_in_dim(path_weight, slot_start, SLOTS_TILE, 0)
        live_slots = (slot_ids < entry_count[tile_index]).astype(jnp.float32)
        picked = jnp.take(tile_patch, slot_rows, axis=1)
        partial_value = jnp.einsum('mkc,kcr->kmr', picked.astype(jnp.float32), slot_weights.astype(jnp.float32), precision=highest)
        slot_select = (slot_blocks[None, :] == block_ids[:, None]).astype(jnp.float32) * live_slots[None, :]
        summed = jnp.einsum('bk,kmr->mbr', slot_select, partial_value, precision=highest).reshape(SAMPLE_TOTAL, rays_column)
        ray_start = (lon_pos * rays_column).astype(jnp.int32)
        current = lax.dynamic_slice_in_dim(ray_total, ray_start, rays_column, 1)
        return (lax.dynamic_update_slice_in_dim(ray_total, current + summed, ray_start, 1), None)
    prior_samples_in_path_space, _ = lax.scan(tile_step, jnp.zeros((SAMPLE_TOTAL, RAYS), jnp.float32), jnp.arange(TILES, dtype=jnp.int32))
    ray_mean = lax.optimization_barrier(jnp.mean(prior_samples_in_path_space, axis=0))
    spread = prior_samples_in_path_space - ray_mean
    misfit = observed - ray_mean
    scaled_innovation = misfit / jnp.sqrt(obs_var)
    gram_sum = jnp.dot(spread / obs_var, spread.T, precision=highest)
    pull_sum = jnp.dot(spread, misfit / obs_var, precision=highest)
    transform = analysis_weights(gram_sum, pull_sum)
    raveled_grid_vector = prior_sample_set.reshape(SAMPLE_TOTAL, -1)
    centre = lax.optimization_barrier(jnp.mean(raveled_grid_vector, axis=0))
    anomalies = raveled_grid_vector - centre
    updated_samples = centre + jnp.dot(transform.T, anomalies, precision=highest)
    return (updated_samples.reshape(prior_sample_set.shape), prior_samples_in_path_space, scaled_innovation)
```

```python
import functools
import math

import jax
import jax.numpy as jnp
from jax import lax
from jax.experimental import pallas as pl
from jax.experimental.pallas import tpu as pltpu
from jax.sharding import PartitionSpec as P

SUB = 8
F32 = jnp.float32
BF16 = jnp.bfloat16
VMEM = pltpu.VMEM
SMEM = pltpu.SMEM
ANY = pl.ANY


def lanes_of(shape):
    return lax.broadcasted_iota(jnp.int32, shape, 1)


def subs_of(shape):
    return lax.broadcasted_iota(jnp.int32, shape, 0)


def pack_kernel(dims, chunks, x_hbm, e_hbm, n_hbm, p_hbm, d_hbm, north_hbm, south_hbm, edge_hbm,
                xs, fields, north, south, edge, in_sem, field_sem, out_sem):
    members, levels, rows, width = dims
    per = levels // chunks
    step = width // levels
    field_refs = (e_hbm, n_hbm, p_hbm, d_hbm)

    def load(c):
        return pltpu.make_async_copy(x_hbm.at[:, pl.ds(c * per, per)], xs.at[c], in_sem.at[c])

    def load_field(f):
        return pltpu.make_async_copy(field_refs[f], fields.at[f], field_sem.at[f])

    for f in range(4):
        load_field(f).start()
    for c in range(chunks):
        load(c).start()
    lane = lanes_of((SUB, width))
    level_of = ((lane + 2) // step) % levels
    edge[...] = jnp.zeros_like(edge)
    for f in range(4):
        load_field(f).wait()
    state_rows = 2 * levels * members
    for f in range(4):
        flat = fields.at[f]
        north[pl.ds(state_rows + f * levels, levels), :] = flat[pl.ds(rows - 1, levels, stride=rows), :]
        south[pl.ds(state_rows + f * levels, levels), :] = flat[pl.ds(0, levels, stride=rows), :]
        acc = jnp.zeros((SUB, width), F32)
        for l in range(levels):
            v = flat[pl.ds(l * rows, rows), :]
            acc = jnp.where(level_of == l, pltpu.roll(v, (step * l) % width, 1), acc)
        edge[pl.ds(rows * members + f * rows, rows), :] = acc

    def send(ref, hbm, c, k):
        part = pl.ds(c * per * 2 * members, per * 2 * members)
        return pltpu.make_async_copy(ref.at[part], hbm.at[part], out_sem.at[k, c])

    def send_tail(ref, hbm, k):
        part = pl.ds(state_rows, 4 * levels)
        return pltpu.make_async_copy(ref.at[part], hbm.at[part], out_sem.at[k, chunks])

    send_tail(north, north_hbm, 0).start()
    send_tail(south, south_hbm, 1).start()
    for c in range(chunks):
        load(c).wait()
        flat = xs.at[c].reshape(members * per * rows, width)

        def group(g, carry):
            for y in range(rows):
                at = pl.ds(pl.multiple_of(y * members + g * SUB, SUB), SUB)
                acc = edge[at, :]
                for li in range(per):
                    l = c * per + li
                    v = flat[pl.ds(g * SUB * per * rows + li * rows + y, SUB, stride=per * rows), :]
                    acc = jnp.where(level_of == l, pltpu.roll(v, (step * l) % width, 1), acc)
                    if y < 2:
                        south[pl.ds(pl.multiple_of((l * 2 + y) * members + g * SUB, SUB), SUB), :] = v
                    if y >= rows - 2:
                        north[pl.ds(pl.multiple_of((l * 2 + y - rows + 2) * members + g * SUB, SUB), SUB), :] = v
                edge[at, :] = acc
            return carry

        lax.fori_loop(0, members // SUB, group, 0)
        send(north, north_hbm, c, 0).start()
        send(south, south_hbm, c, 1).start()
    last = pltpu.make_async_copy(edge, edge_hbm, out_sem.at[2, 0])
    last.start()
    for c in range(chunks):
        send(north, north_hbm, c, 0).wait()
        send(south, south_hbm, c, 1).wait()
    send_tail(north, north_hbm, 0).wait()
    send_tail(south, south_hbm, 1).wait()
    last.wait()


def pack(x, fields, chunks=4):
    members, levels, rows, width = x.shape
    halo = 2 * levels * members + 4 * levels
    edge = rows * members + 4 * rows
    per = levels // chunks
    return pl.pallas_call(
        functools.partial(pack_kernel, x.shape, chunks),
        name="pack_halos",
        out_shape=(
            jax.ShapeDtypeStruct((halo, width), F32),
            jax.ShapeDtypeStruct((halo, width), F32),
            jax.ShapeDtypeStruct((edge, width), F32),
        ),
        in_specs=[pl.BlockSpec(memory_space=ANY)] * 5,
        out_specs=[pl.BlockSpec(memory_space=ANY)] * 3,
        scratch_shapes=[
            VMEM((chunks, members, per, rows, width), F32),
            VMEM((4, levels * rows, width), F32),
            VMEM((halo, width), F32),
            VMEM((halo, width), F32),
            VMEM((edge, width), F32),
            pltpu.SemaphoreType.DMA((chunks,)),
            pltpu.SemaphoreType.DMA((4,)),
            pltpu.SemaphoreType.DMA((3, chunks + 1)),
        ],
        cost_estimate=pl.CostEstimate(flops=4_000_000, bytes_accessed=8_000_000, transcendentals=0),
    )(x, *fields)


def stencil(e, n, p, d):
    keep = 1.0 - d
    ep, em = jnp.maximum(e, 0.0), jnp.minimum(e, 0.0)
    np_, nm = jnp.maximum(n, 0.0), jnp.minimum(n, 0.0)
    return (
        keep * (1.0 - ep + em - np_ + nm),
        keep * ep,
        -(keep * em),
        keep * np_,
        -(keep * nm),
        p,
    )


def forecast_kernel(dims, per, lat_size, slots, blocks_dev,
                    slot_of, row_of, count,
                    x_ref, below_ref, above_ref, belowc_ref, abovec_ref,
                    e_ref, n_ref, p_ref, d_ref,
                    edge, west, east, corner_s, corner_n, pw_hbm,
                    f_ref, *rest):
    members, levels, rows, width = dims
    outs, (halo, halo1, coef, strip, content, content16, rays, pw, pw_sem) = rest[:lat_size], rest[lat_size:]
    step_id = pl.program_id(0)
    groups = members // SUB
    step = width // levels
    lane = lanes_of((SUB, width))
    first, final = lane == 0, lane == width - 1
    from_west = ((lane + 2) % step) < 2
    tall = 2 * rows

    def tile(ref, start):
        return ref[pl.ds(pl.multiple_of(start, SUB), SUB), :]

    def spread(ref, k, row):
        return ref[k, pl.ds(row, SUB, stride=0), :]

    @pl.when(step_id == 0)
    def _():
        pltpu.make_async_copy(pw_hbm, pw, pw_sem).start()
        for g in range(groups):
            halo[pl.ds(g * SUB, SUB), :] = corner_s[pl.ds(g * SUB, SUB), :]
            halo[pl.ds((rows + 1) * members + g * SUB, SUB), :] = corner_n[pl.ds(g * SUB, SUB), :]
            for y in range(rows):
                at = pl.ds(y * members + g * SUB, SUB)
                halo[pl.ds((y + 1) * members + g * SUB, SUB), :] = jnp.where(from_west, west[at, :], east[at, :])
        merged = []
        for f in range(4):
            at = pl.ds(rows * members + f * rows, rows)
            merged.append(jnp.where(from_west, west[at, :], east[at, :]))
        for k, c in enumerate(stencil(*merged)):
            strip[k] = c
        for y in range(rows):
            c0, cw, ce, cs, cn, p = [spread(strip, k, y) for k in range(6)]
            for g in range(groups):
                at = pl.ds(y * members + g * SUB, SUB)
                own, aw, ae = edge[at, :], west[at, :], east[at, :]
                side_w = jnp.where(from_west, pltpu.roll(aw, 1, 1), pltpu.roll(own, 1, 1))
                side_e = jnp.where(from_west, pltpu.roll(own, width - 1, 1), pltpu.roll(ae, width - 1, 1))
                mid = halo[pl.ds((y + 1) * members + g * SUB, SUB), :]
                low = halo[pl.ds(y * members + g * SUB, SUB), :]
                high = halo[pl.ds((y + 2) * members + g * SUB, SUB), :]
                halo1[at, :] = (c0 * mid + cw * side_w) + (ce * side_e + cs * low) + (cn * high + p)
        content[...] = jnp.zeros_like(content)

    here = [r[...] for r in (e_ref, n_ref, p_ref, d_ref)]
    for li in range(per):
        part = slice(li * rows, (li + 1) * rows)
        for k, c in enumerate(stencil(*[h[part] for h in here])):
            coef[k, pl.ds(li * tall, rows), :] = c
    base = pl.multiple_of(step_id * per, per)
    for source, row in ((abovec_ref, rows), (belowc_ref, rows + 1)):
        got = [source[pl.ds(f * levels + base, per), :] for f in range(4)]
        for k, c in enumerate(stencil(*got)):
            coef[k, pl.ds(row, per, stride=tall), :] = c
    flat = x_ref.reshape(members * per * rows, width)

    def level(li, carry):
        l = base + li
        turn = (width - step * l) % width

        def coefs(y):
            row = li * tall + (y if y >= 0 else rows + 1)
            return [spread(coef, k, row) for k in range(6)]

        def start_row(y):
            if y < 0:
                return [tile(below_ref, (li * 2 + y + 2) * members + g * SUB) for g in range(groups)]
            if y >= rows:
                return [tile(above_ref, (li * 2 + y - rows) * members + g * SUB) for g in range(groups)]
            return [
                flat[pl.ds(g * SUB * per * rows + li * rows + y, SUB, stride=per * rows), :]
                for g in range(groups)
            ]

        def advance(mid, low, high, side, c):
            c0, cw, ce, cs, cn, p = c
            out = []
            for g in range(groups):
                edge_values = pltpu.roll(side[g], turn, 1)
                v = mid[g]
                w = pltpu.roll(jnp.where(final, edge_values, v), 1, 1)
                e = pltpu.roll(jnp.where(first, edge_values, v), width - 1, 1)
                out.append((c0 * v + cw * w) + (ce * e + cs * low[g]) + (cn * high[g] + p))
            return out

        before, now = start_row(-2), start_row(-1)
        older, old, older_c = None, None, None
        for y in range(-1, rows + 1):
            after = start_row(y + 1)
            c = coefs(y)
            side = [tile(halo, (y + 1) * members + g * SUB) for g in range(groups)]
            new = advance(now, before, after, side, c)
            if older is not None:
                y2 = y - 1
                side1 = [tile(halo1, y2 * members + g * SUB) for g in range(groups)]
                done = advance(old, older, new, side1, older_c)
                for g in range(groups):
                    at = pl.ds(y2 * members + g * SUB, SUB)
                    content[at, :] += done[g]
                    f_ref[pl.ds(pl.multiple_of((li * rows + y2) * members + g * SUB, SUB), SUB), :] = done[g]
            older, old, older_c = old, new, c
            before, now = now, after
        return carry

    lax.fori_loop(0, per, level, 0)

    @pl.when(step_id == pl.num_programs(0) - 1)
    def _():
        content16[...] = (content[...] / math.sqrt(levels)).astype(BF16)
        rays[...] = jnp.zeros_like(rays)
        pltpu.make_async_copy(pw_hbm, pw, pw_sem).wait()
        live = count[0]
        for k in range(slots):
            picked = content16[pl.ds(pl.multiple_of(row_of[k] * members, members), members), :]
            partial = jnp.dot(picked, pw[k], preferred_element_type=F32)
            partial = jnp.where(k < live, partial, 0.0)
            at = pl.ds(pl.multiple_of(slot_of[k] * members, members), members)
            rays[at, :] += partial
        size = blocks_dev * members
        for s in range(lat_size):
            outs[s][...] = rays[pl.ds(s * size, size), :]


def forecast(x, fields, below, above, edge, west, east, corner_s, corner_n, pw, slot_of, row_of, count,
             lat_size, blocks_dev, per=4):
    members, levels, rows, width = x.shape
    slots, _, block = pw.shape
    halo_rows = per * 2 * members
    tail = (2 * levels * members) // (4 * levels)
    whole = lambda shape: pl.BlockSpec(shape, lambda i: (0,) * len(shape))
    smem = pl.BlockSpec(memory_space=SMEM)
    field = pl.BlockSpec((per * rows, width), lambda i: (i, 0))
    size = blocks_dev * members
    return pl.pallas_call(
        functools.partial(forecast_kernel, x.shape, per, lat_size, slots, blocks_dev),
        name="forecast_rays",
        grid=(levels // per,),
        out_shape=[jax.ShapeDtypeStruct((levels * rows * members, width), F32)]
        + [jax.ShapeDtypeStruct((size, block), F32)] * lat_size,
        in_specs=[smem, smem, smem,
                  pl.BlockSpec((members, per, rows, width), lambda i: (0, i, 0, 0)),
                  pl.BlockSpec((halo_rows, width), lambda i: (i, 0)),
                  pl.BlockSpec((halo_rows, width), lambda i: (i, 0)),
                  pl.BlockSpec((4 * levels, width), lambda i: (tail, 0)),
                  pl.BlockSpec((4 * levels, width), lambda i: (tail, 0)),
                  field, field, field, field,
                  whole(edge.shape), whole(edge.shape), whole(edge.shape),
                  whole(corner_s.shape), whole(corner_s.shape),
                  pl.BlockSpec(memory_space=ANY)],
        out_specs=[pl.BlockSpec((per * rows * members, width), lambda i: (i, 0))] + [whole((size, block))] * lat_size,
        scratch_shapes=[
            VMEM(((rows + 2) * members, width), F32),
            VMEM((rows * members, width), F32),
            VMEM((6, per * 2 * rows, width), F32),
            VMEM((6, rows, width), F32),
            VMEM((rows * members, width), F32),
            VMEM((rows * members, width), BF16),
            VMEM((lat_size * size, block), F32),
            VMEM(pw.shape, BF16),
            pltpu.SemaphoreType.DMA,
        ],
        cost_estimate=pl.CostEstimate(flops=60_000_000, bytes_accessed=12_000_000, transcendentals=0),
    )(slot_of, row_of, count, x, below, above, below, above, *fields, edge, west, east, corner_s, corner_n, pw)


def spread_kernel(members, rows, width, pairs, f_ref, hi_ref, lo_ref, centre_ref):
    sub = subs_of((rows, width))
    for q in range(pairs):
        for h in range(2):
            mean = jnp.zeros((rows, width), F32)
            for y in range(rows):
                at = ((q * 2 + h) * rows + y) * members
                v = f_ref[pl.ds(at, members), :]
                m = jnp.sum(v, axis=0, keepdims=True) / members
                mean = jnp.where(sub == y, m, mean)
                a = v - m
                hi = a.astype(BF16)
                to = (q, pl.ds(y * members, members), pl.ds(h * width, width))
                hi_ref[to] = hi
                lo_ref[to] = (a - hi.astype(F32)).astype(BF16)
            centre_ref[pl.ds((q * 2 + h) * rows, rows), :] = mean


def anomalies(f, members, levels, rows, width, pairs=2):
    shape = (levels // 2, rows * members, 2 * width)
    block = (pairs, rows * members, 2 * width)
    return pl.pallas_call(
        functools.partial(spread_kernel, members, rows, width, pairs),
        name="anomalies",
        grid=(levels // 2 // pairs,),
        out_shape=(jax.ShapeDtypeStruct(shape, BF16), jax.ShapeDtypeStruct(shape, BF16),
                   jax.ShapeDtypeStruct((levels * rows, width), F32)),
        in_specs=[pl.BlockSpec((pairs * 2 * rows * members, width), lambda i: (i, 0))],
        out_specs=[pl.BlockSpec(block, lambda i: (i, 0, 0)), pl.BlockSpec(block, lambda i: (i, 0, 0)),
                   pl.BlockSpec((pairs * 2 * rows, width), lambda i: (i, 0))],
        cost_estimate=pl.CostEstimate(flops=8_000_000, bytes_accessed=8_000_000, transcendentals=0),
    )(f)


def moments_kernel(members, blocks_dev, block, n_parts, *refs):
    parts, (obs_ref, var_ref, prior_ref, innov_ref, packed_ref) = refs[:n_parts], refs[n_parts:]
    scaled, both = [], []
    for b in range(blocks_dev):
        at = pl.ds(b * members, members)
        total = parts[0][at, :]
        for part in parts[1:]:
            total = total + part[at, :]
        prior_ref[:, pl.ds(b * block, block)] = total
        mean = jnp.sum(total, axis=0, keepdims=True) / members
        dev = total - mean
        var = var_ref[pl.ds(b, 1), :]
        misfit = obs_ref[pl.ds(b, 1), :] - mean
        innov_ref[pl.ds(b, 1), :] = misfit / jnp.sqrt(var)
        scaled.append(dev / var)
        both.append(jnp.concatenate([dev, jnp.broadcast_to(misfit, (SUB, block))], axis=0))
    left = jnp.concatenate(scaled, axis=1)
    right = jnp.concatenate(both, axis=1)
    g = lax.dot_general(left, right, (((1,), (1,)), ((), ())), precision=lax.Precision.HIGHEST,
                        preferred_element_type=F32)
    wide = jnp.concatenate([g, jnp.zeros((members, 128 - g.shape[1]), F32)], axis=1)
    lane = lanes_of((SUB, 128))
    packed = jnp.zeros((SUB, 128), F32)
    groups = members // SUB
    start = 0
    for i in range(groups):
        v = wide[i * SUB:(i + 1) * SUB]
        stop = start + SUB * (i + 1)
        moved = pltpu.roll(v, start, 1) if start else v
        packed = jnp.where((lane >= start) & (lane < stop), moved, packed)
        start = stop
    for i in range(groups):
        v = wide[i * SUB:(i + 1) * SUB]
        packed = jnp.where(lane == start + i, pltpu.roll(v, start + i - members, 1), packed)
    packed_ref[...] = packed


def moments(parts, obs, var, members, blocks_dev, block):
    whole = pl.BlockSpec(memory_space=VMEM)
    return pl.pallas_call(
        functools.partial(moments_kernel, members, blocks_dev, block, len(parts)),
        name="moments",
        out_shape=(jax.ShapeDtypeStruct((members, blocks_dev * block), F32),
                   jax.ShapeDtypeStruct((blocks_dev, block), F32),
                   jax.ShapeDtypeStruct((SUB, 128), F32)),
        in_specs=[whole] * (len(parts) + 2),
        out_specs=[whole] * 3,
        cost_estimate=pl.CostEstimate(flops=4_000_000, bytes_accessed=400_000, transcendentals=0),
    )(*parts, obs, var)


def weights(gathered, members, devices):
    groups = members // SUB
    lane = lanes_of((SUB, 128))
    sub = subs_of((SUB, 128))
    total = gathered[pl.ds(0, SUB), :]
    for d in range(1, devices):
        total = total + gathered[pl.ds(d * SUB, SUB), :]
    lower, start = [], 0
    for i in range(groups):
        v = pltpu.roll(total, (128 - start) % 128, 1) if start else total
        lower.append(jnp.where(lane < SUB * (i + 1), v, 0.0))
        start += SUB * (i + 1)
    upper = jnp.transpose(jnp.concatenate(lower, axis=0))
    upper = upper[:members]
    upper = jnp.concatenate([upper, jnp.zeros((members, 128 - members), F32)], axis=1)
    rows = []
    for i in range(groups):
        a = jnp.where(lane < SUB * (i + 1), lower[i], upper[i * SUB:(i + 1) * SUB])
        a = jnp.where(lane < members, a, 0.0)
        a = a + jnp.where(lane == sub + SUB * i, members - 1.0, 0.0)
        a = jnp.where(lane == members + sub + SUB * i, 1.0, a)
        pull = pltpu.roll(total, (2 * members - start - i) % 128, 1)
        rows.append(jnp.where(lane == 2 * members, pull, a))
    for k in range(members):
        i0, s = divmod(k, SUB)
        pivot_row = jnp.broadcast_to(rows[i0][s:s + 1, :], (SUB, 128))
        pivot = jnp.broadcast_to(pivot_row[:, k:k + 1], (SUB, 128))
        ratio = pivot_row / pivot
        for i in range(i0, groups):
            if i == i0 and s == SUB - 1:
                continue
            factor = jnp.broadcast_to(rows[i][:, k:k + 1], (SUB, 128))
            if i == i0:
                factor = jnp.where(sub > s, factor, 0.0)
            rows[i] = rows[i] - factor * ratio
    mean_weight = jnp.zeros((SUB, 128), F32)
    for i in range(groups):
        pivot = jnp.sum(jnp.where(lane == sub + SUB * i, rows[i], 0.0), axis=1, keepdims=True)
        rows[i] = rows[i] / jnp.sqrt(pivot)
        mean_weight = mean_weight + rows[i] * rows[i][:, 2 * members:2 * members + 1]
    mean_weight = jnp.sum(mean_weight, axis=0, keepdims=True)
    return [mean_weight + math.sqrt(members - 1.0) * r for r in rows]


def update_kernel(dims, devices, pairs, gathered, hi_ref, lo_ref, centre_ref, out_ref, mat_hi, mat_lo):
    members, levels, rows, width = dims
    size = rows * members

    @pl.when(pl.program_id(0) == 0)
    def _():
        lane = lanes_of((rows, 128))
        sub = subs_of((rows, 128))
        copies = 128 // members
        made = weights(gathered, members, devices)
        for i, r in enumerate(made):
            r = jnp.where(lane < members, pltpu.roll(r, 128 - members, 1), 0.0)
            tiled = r
            for q in range(1, copies):
                tiled = tiled + pltpu.roll(r, q * members, 1)
            for s in range(0, SUB, 2):
                b = i * SUB + s
                for h in range(size // 128):
                    keep = (lane // members) + h * copies == sub
                    two = [jnp.where(keep, jnp.broadcast_to(tiled[t:t + 1], (rows, 128)), 0.0) for t in (s, s + 1)]
                    m = jnp.concatenate(two, axis=0)
                    big = m.astype(BF16)
                    to = (pl.ds(b * rows, 2 * rows), pl.ds(h * 128, 128))
                    mat_hi[to] = big
                    mat_lo[to] = (m - big.astype(F32)).astype(BF16)

    for q in range(pairs):
        hi, lo = hi_ref[q], lo_ref[q]
        big = mat_hi[...]
        dot = functools.partial(jnp.dot, preferred_element_type=F32)
        acc = dot(big, hi) + dot(big, lo) + dot(mat_lo[...], hi)
        for h in range(2):
            centre = centre_ref[pl.ds((q * 2 + h) * rows, rows), :]
            part = acc[:, h * width:(h + 1) * width].reshape(members, rows, width)
            out_ref[:, q * 2 + h] = part + centre[None]


def update(gathered, hi, lo, centre, dims, devices, pairs=2):
    members, levels, rows, width = dims
    block = (pairs, rows * members, 2 * width)
    return pl.pallas_call(
        functools.partial(update_kernel, dims, devices, pairs),
        name="update",
        grid=(levels // 2 // pairs,),
        out_shape=jax.ShapeDtypeStruct(dims, F32),
        in_specs=[pl.BlockSpec(gathered.shape, lambda i: (0, 0)),
                  pl.BlockSpec(block, lambda i: (i, 0, 0)), pl.BlockSpec(block, lambda i: (i, 0, 0)),
                  pl.BlockSpec((pairs * 2 * rows, width), lambda i: (i, 0))],
        out_specs=pl.BlockSpec((members, pairs * 2, rows, width), lambda i: (0, i, 0, 0)),
        scratch_shapes=[VMEM((rows * members, rows * members), BF16)] * 2,
        cost_estimate=pl.CostEstimate(flops=2_000_000_000, bytes_accessed=8_000_000, transcendentals=0),
    )(gathered, hi, lo, centre)


def per_device(sample_deviations, east_courant, north_courant, production, loss_rate, entry_count, entry_row,
               entry_block, path_weight, observed, obs_var):
    dims = members, levels, rows, width = sample_deviations.shape
    lat_size, lon_size = lax.axis_size("lat"), lax.axis_size("lon")
    block = path_weight.shape[2]
    blocks_dev = observed.shape[0] // block
    step = width // levels
    ring = lambda n, s: [(i, (i + s) % n) for i in range(n)]
    up = [(i, i + 1) for i in range(lat_size - 1)]
    down = [(j, i) for i, j in up]

    fields = [f.reshape(levels * rows, width) for f in (east_courant, north_courant, production, loss_rate)]
    to_north, to_south, edge = pack(sample_deviations, fields)
    below = lax.ppermute(to_north, "lat", up)
    above = lax.ppermute(to_south, "lat", down)
    west = lax.ppermute(edge, "lon", ring(lon_size, 1))
    east = lax.ppermute(edge, "lon", ring(lon_size, lon_size - 1))
    from_west = ((jnp.arange(width) + 2) % step < 2)[None, :]
    top = slice((rows - 1) * members, rows * members)
    corner_s = lax.ppermute(jnp.where(from_west, west[top], east[top]), "lat", up)
    corner_n = lax.ppermute(jnp.where(from_west, west[:members], east[:members]), "lat", down)

    mine = lax.axis_index("lat")
    slot_of = ((entry_block // blocks_dev - mine) % lat_size) * blocks_dev + entry_block % blocks_dev
    f, *sums = forecast(sample_deviations, fields, below, above, edge, west, east, corner_s, corner_n, path_weight,
                        slot_of, entry_row, entry_count, lat_size, blocks_dev)
    got = [sums[0]] + [lax.ppermute(sums[s], "lat", ring(lat_size, s)) for s in range(1, lat_size)]
    hi, lo, centre = anomalies(f, members, levels, rows, width)
    prior, innovation, packed = moments(got, observed.reshape(blocks_dev, block), obs_var.reshape(blocks_dev, block),
                                        members, blocks_dev, block)
    devices = lat_size * lon_size
    spread_out = jnp.broadcast_to(packed[None], (devices, SUB, 128)).reshape(devices * SUB, 128)
    gathered = lax.all_to_all(spread_out, ("lon", "lat"), 0, 0, tiled=True)
    updated = update(gathered, hi, lo, centre, dims, devices)
    return updated, prior, innovation.reshape(observed.shape)


def solution(mesh):
    tile = P(None, "lat", "lon")
    owned = P(("lon", "lat"))
    in_specs = (P(None, None, "lat", "lon"), tile, tile, tile, tile, owned, owned, owned,
                P(("lon", "lat"), None, None), owned, owned)
    out_specs = (P(None, None, "lat", "lon"), P(None, ("lon", "lat")), owned)
    return jax.shard_map(per_device, mesh=mesh, in_specs=in_specs, out_specs=out_specs, check_vma=False)
```

```python
import functools
import math

import jax
import jax.numpy as jnp
from jax import lax
from jax.experimental import pallas as pl
from jax.experimental.pallas import tpu as pltpu
from jax.sharding import PartitionSpec as P


SUB = 8
F32 = jnp.float32
BF16 = jnp.bfloat16
VMEM = pltpu.VMEM
SMEM = pltpu.SMEM


def lanes_of(shape):
    return lax.broadcasted_iota(jnp.int32, shape, 1)


def subs_of(shape):
    return lax.broadcasted_iota(jnp.int32, shape, 0)


def grant(mib, flops, moved):
    return dict(
        compiler_params=pltpu.CompilerParams(vmem_limit_bytes=mib * 1024 * 1024),
        cost_estimate=pl.CostEstimate(flops=flops, bytes_accessed=moved, transcendentals=0),
    )


def near(*arrays):
    return [pltpu.with_memory_space_constraint(a, pltpu.VMEM) for a in arrays]


def far(*arrays):
    return [pltpu.with_memory_space_constraint(a, pltpu.HBM) for a in arrays]


IN_VMEM = pl.BlockSpec(memory_space=VMEM)
IN_SMEM = pl.BlockSpec(memory_space=SMEM)
IN_HBM = pl.BlockSpec(memory_space=pltpu.HBM)


def pack_kernel(dims, chunks, x_hbm, e_hbm, n_hbm, p_hbm, d_hbm, state, north, south, edge, fields,
                in_sem, field_sem, tail_sem):
    members, levels, rows, width = dims
    per = levels // chunks
    step = width // levels
    field_refs = (e_hbm, n_hbm, p_hbm, d_hbm)
    state_rows = 2 * levels * members

    def load(l, y):
        return pltpu.make_async_copy(x_hbm.at[:, l, y], state.at[l * rows + y], in_sem.at[l // per])

    def load_field(f):
        return pltpu.make_async_copy(field_refs[f], fields.at[f], field_sem.at[f])

    for f in range(4):
        load_field(f).start()
    for l in range(levels):
        for y in range(rows):
            load(l, y).start()
    lane = lanes_of((SUB, width))
    level_of = ((lane + 2) // step) % levels
    edge[...] = jnp.zeros_like(edge)
    for f in range(4):
        load_field(f).wait()
        acc = jnp.zeros((SUB, width), F32)
        for l in range(levels):
            acc = jnp.where(level_of == l, pltpu.roll(fields[f, l], (step * l) % width, 1), acc)
        edge[pl.ds(rows * members + f * rows, rows), :] = acc
        at = pl.ds(state_rows + f * levels, levels)
        pltpu.make_async_copy(fields.at[f, :, rows - 1], north.at[at], tail_sem.at[0, f]).start()
        pltpu.make_async_copy(fields.at[f, :, 0], south.at[at], tail_sem.at[1, f]).start()
    for c in range(chunks):
        first = c * per
        for l in range(first, first + per):
            for y in range(rows):
                load(l, y).wait()
        for l in range(first, first + per):
            for r in range(2):
                at = pl.ds((l * 2 + r) * members, members)
                south[at, :] = state[l * rows + r]
                north[at, :] = state[l * rows + rows - 2 + r]
        for y in range(rows):
            for g in range(members // SUB):
                at = pl.ds(y * members + g * SUB, SUB)
                acc = edge[at, :]
                for l in range(first, first + per):
                    v = state[l * rows + y, pl.ds(g * SUB, SUB), :]
                    acc = jnp.where(level_of == l, pltpu.roll(v, (step * l) % width, 1), acc)
                edge[at, :] = acc
    for f in range(4):
        at = pl.ds(state_rows + f * levels, levels)
        pltpu.make_async_copy(fields.at[f, :, rows - 1], north.at[at], tail_sem.at[0, f]).wait()
        pltpu.make_async_copy(fields.at[f, :, 0], south.at[at], tail_sem.at[1, f]).wait()


def pack(x, fields, chunks=4):
    members, levels, rows, width = x.shape
    halo = 2 * levels * members + 4 * levels
    edge = rows * members + 4 * rows
    return pl.pallas_call(
        functools.partial(pack_kernel, x.shape, chunks),
        name="pack_halos",
        out_shape=(
            VMEM((levels * rows, members, width), F32),
            VMEM((halo, width), F32),
            VMEM((halo, width), F32),
            VMEM((edge, width), F32),
            VMEM((4, levels, rows, width), F32),
        ),
        in_specs=[IN_HBM] * 5,
        out_specs=[IN_VMEM] * 5,
        scratch_shapes=[
            pltpu.SemaphoreType.DMA((chunks,)),
            pltpu.SemaphoreType.DMA((4,)),
            pltpu.SemaphoreType.DMA((2, 4)),
        ],
        **grant(8, 4_000_000, 8_000_000),
    )(*far(x, *fields))


def stencil(e, n, p, d):
    keep = 1.0 - d
    ep, em = jnp.maximum(e, 0.0), jnp.minimum(e, 0.0)
    np_, nm = jnp.maximum(n, 0.0), jnp.minimum(n, 0.0)
    return (
        keep * (1.0 - ep + em - np_ + nm),
        keep * ep,
        -(keep * em),
        keep * np_,
        -(keep * nm),
        p,
    )


def sided(side, turn, v, width):
    lane = lanes_of(v.shape)
    values = pltpu.roll(side, turn, 1)
    w = pltpu.roll(jnp.where(lane == width - 1, values, v), 1, 1)
    e = pltpu.roll(jnp.where(lane == 0, values, v), width - 1, 1)
    return w, e


def advance(mid, low, high, side, turn, c, width):
    c0, cw, ce, cs, cn, p = c
    out = []
    for g, v in enumerate(mid):
        w, e = sided(side[g], turn, v, width)
        total = (c0 * v + cw * w) + (ce * e + p)
        if low is not None:
            total = total + cs * low[g]
        if high is not None:
            total = total + cn * high[g]
        out.append(total)
    return out


def spread(ref, k, row):
    return ref[k, pl.ds(row, SUB, stride=0), :]


def interior_kernel(dims, state, fields, edge, west, east, pw_hbm,
                    inner, part, content, coef, halo1, strip, pw, halo, pw_sem):
    members, levels, rows, width = dims
    fetch = pltpu.make_async_copy(pw_hbm, pw, pw_sem)
    fetch.start()
    groups = members // SUB
    step = width // levels
    from_west = ((lanes_of((SUB, width)) + 2) % step) < 2
    merged = []
    for f in range(4):
        at = pl.ds(rows * members + f * rows, rows)
        merged.append(jnp.where(from_west, west[at, :], east[at, :]))
    for k, c in enumerate(stencil(*merged)):
        strip[k] = c
    for y in range(rows):
        for g in range(groups):
            at = pl.ds(y * members + g * SUB, SUB)
            halo[at, :] = jnp.where(from_west, west[at, :], east[at, :])
    for y in range(rows):
        c0, cw, ce, cs, cn, p = [spread(strip, k, y) for k in range(6)]
        for g in range(groups):
            at = pl.ds(y * members + g * SUB, SUB)
            own, aw, ae = edge[at, :], west[at, :], east[at, :]
            side_w = jnp.where(from_west, pltpu.roll(aw, 1, 1), pltpu.roll(own, 1, 1))
            side_e = jnp.where(from_west, pltpu.roll(own, width - 1, 1), pltpu.roll(ae, width - 1, 1))
            total = (c0 * halo[at, :] + cw * side_w) + (ce * side_e + p)
            if y > 0:
                total = total + cs * halo[pl.ds((y - 1) * members + g * SUB, SUB), :]
            if y < rows - 1:
                total = total + cn * halo[pl.ds((y + 1) * members + g * SUB, SUB), :]
            halo1[at, :] = total
    content[...] = jnp.zeros_like(content)

    def level(l, carry):
        turn = (width - step * l) % width
        base = pl.multiple_of(l * rows, rows)
        got = stencil(*[fields[f, l] for f in range(4)])
        for k, c in enumerate(got):
            coef[k, pl.ds(base, rows), :] = c

        def load(ref, row):
            return [ref[row, pl.ds(g * SUB, SUB), :] for g in range(groups)]

        def sides(ref, y):
            return [ref[pl.ds(y * members + g * SUB, SUB), :] for g in range(groups)]

        def store(ref, row, values):
            for g in range(groups):
                ref[row, pl.ds(g * SUB, SUB), :] = values[g]

        before, now = None, load(state, base)
        older, old, older_c = None, None, None
        for y in range(rows):
            after = load(state, base + y + 1) if y < rows - 1 else None
            c = [spread(coef, k, base + y) for k in range(6)]
            new = advance(now, before, after, sides(halo, y), turn, c, width)
            if y in (0, 1, rows - 2, rows - 1):
                store(part, l * 6 + {0: 0, 1: 1, rows - 2: 2, rows - 1: 3}[y], new)
            y2 = y - 1
            if y2 >= 1:
                done = advance(old, older if y2 > 1 else None, new if y2 < rows - 2 else None,
                               sides(halo1, y2), turn, older_c, width)
                if y2 == 1:
                    store(part, l * 6 + 4, done)
                elif y2 == rows - 2:
                    store(part, l * 6 + 5, done)
                else:
                    store(inner, l * (rows - 4) + y2 - 2, done)
                    for g in range(groups):
                        content[pl.ds((y2 - 2) * members + g * SUB, SUB), :] += done[g]
            older, old, older_c = old, new, c
            before, now = now, after
        return carry

    lax.fori_loop(0, levels, level, 0)
    fetch.wait()


def interior(dims, state, fields, edge, west, east, pw):
    members, levels, rows, width = dims
    shapes = (
        (levels * (rows - 4), members, width),
        (levels * 6, members, width),
        ((rows - 4) * members, width),
        (6, levels * rows, width),
        (rows * members, width),
        (6, rows, width),
    )
    return pl.pallas_call(
        functools.partial(interior_kernel, dims),
        name="interior",
        out_shape=[VMEM(s, F32) for s in shapes] + [VMEM(pw.shape, BF16)],
        in_specs=[IN_VMEM] * 5 + [IN_HBM],
        out_specs=[IN_VMEM] * 7,
        scratch_shapes=[VMEM((rows * members, width), F32), pltpu.SemaphoreType.DMA],
        **grant(8, 60_000_000, 12_000_000),
    )(*near(state, fields, edge, west, east), *far(pw))


def boundary_kernel(dims, lat_size, slots, blocks_dev, block_of, row_of, count,
                    state, part, inner_content, coef, halo1, strip, pw, corner_s, corner_n, below, above,
                    outer, *rest):
    members, levels, rows, width = dims
    outs, (low_coef, high_coef, content, content16, rays, ends) = rest[:lat_size], rest[lat_size:]
    groups = members // SUB
    step = width // levels
    tail = 2 * levels * members
    for source, target in ((below, low_coef), (above, high_coef)):
        got = [source[pl.ds(tail + f * levels, levels), :] for f in range(4)]
        for k, c in enumerate(stencil(*got)):
            target[k] = c
    for i, (y, k, corner) in enumerate(((0, 3, corner_s), (rows - 1, 4, corner_n))):
        c = spread(strip, k, y)
        for g in range(groups):
            at = pl.ds(g * SUB, SUB)
            ends[i, at, :] = halo1[pl.ds(y * members + g * SUB, SUB), :] + c * corner[at, :]
    edge_rows = (0, 1, rows - 2, rows - 1)
    for y in edge_rows:
        at = pl.ds(y * members, members)
        content[at, :] = jnp.zeros((members, width), F32)
    content[pl.ds(2 * members, (rows - 4) * members), :] = inner_content[...]

    def level(l, carry):
        turn = (width - step * l) % width
        base = pl.multiple_of(l * rows, rows)

        def halo_row(ref, r):
            start = pl.multiple_of((l * 2 + r) * members, members)
            return [ref[pl.ds(start + g * SUB, SUB), :] for g in range(groups)]

        def load(ref, row):
            return [ref[row, pl.ds(g * SUB, SUB), :] for g in range(groups)]

        def side(ref):
            return [ref[pl.ds(g * SUB, SUB), :] for g in range(groups)]

        def add(partial, c, values):
            return [q + c * v for q, v in zip(partial, values)]

        south1, north1 = halo_row(below, 1), halo_row(above, 0)
        lower = advance(south1, halo_row(below, 0), load(state, base), side(corner_s), turn,
                        [spread(low_coef, k, l) for k in range(6)], width)
        upper = advance(north1, load(state, base + rows - 1), halo_row(above, 1), side(corner_n), turn,
                        [spread(high_coef, k, l) for k in range(6)], width)
        c_first = [spread(coef, k, base) for k in range(6)]
        c_last = [spread(coef, k, base + rows - 1) for k in range(6)]
        first = add(load(part, l * 6), c_first[3], south1)
        last = add(load(part, l * 6 + 3), c_last[4], north1)
        done = (
            advance(first, lower, load(part, l * 6 + 1), side(ends.at[0]), turn, c_first, width),
            add(load(part, l * 6 + 4), spread(coef, 3, base + 1), first),
            add(load(part, l * 6 + 5), spread(coef, 4, base + rows - 2), last),
            advance(last, load(part, l * 6 + 2), upper, side(ends.at[1]), turn, c_last, width),
        )
        for i, y in enumerate(edge_rows):
            for g in range(groups):
                content[pl.ds(y * members + g * SUB, SUB), :] += done[i][g]
                outer[l * 4 + i, pl.ds(g * SUB, SUB), :] = done[i][g]
        return carry

    lax.fori_loop(0, levels, level, 0)
    content16[...] = (content[...] / math.sqrt(levels)).astype(BF16)
    rays[...] = jnp.zeros_like(rays)
    live = count[0]
    mine = lax.axis_index("lat")
    for k in range(slots):
        picked = content16[pl.ds(pl.multiple_of(row_of[k] * members, members), members), :]
        partial = jnp.dot(picked, pw[k], preferred_element_type=F32)
        partial = jnp.where(k < live, partial, 0.0)
        owner = lax.rem(block_of[k] // blocks_dev - mine + lat_size, lat_size)
        place = owner * blocks_dev + lax.rem(block_of[k], blocks_dev)
        at = pl.ds(pl.multiple_of(place * members, members), members)
        rays[at, :] += partial
    size = blocks_dev * members
    for s in range(lat_size):
        outs[s][...] = rays[pl.ds(s * size, size), :]


def boundary(dims, state, inside, corner_s, corner_n, below, above, block_of, row_of, count, lat_size, blocks_dev):
    members, levels, rows, width = dims
    slots, _, block = inside[-1].shape
    size = blocks_dev * members
    return pl.pallas_call(
        functools.partial(boundary_kernel, dims, lat_size, slots, blocks_dev),
        name="boundary_rays",
        out_shape=[VMEM((levels * 4, members, width), F32)] + [VMEM((size, block), F32)] * lat_size,
        in_specs=[IN_SMEM] * 3 + [IN_VMEM] * 11,
        out_specs=[IN_VMEM] * (1 + lat_size),
        scratch_shapes=[
            VMEM((6, levels, width), F32),
            VMEM((6, levels, width), F32),
            VMEM((rows * members, width), F32),
            VMEM((rows * members, width), BF16),
            VMEM((lat_size * size, block), F32),
            VMEM((2, members, width), F32),
        ],
        **grant(8, 30_000_000, 12_000_000),
    )(block_of, row_of, count, *near(state, *inside, corner_s, corner_n, below, above))


def spread_kernel(dims, inner, outer, hi_ref, lo_hbm, centre_ref, lo_ref, sem):
    members, levels, rows, width = dims
    sub = subs_of((rows, width))
    edge_rows = {0: 0, 1: 1, rows - 2: 2, rows - 1: 3}

    def pair(q, carry):
        for h in range(2):
            l = q * 2 + h
            mean = jnp.zeros((rows, width), F32)
            for y in range(rows):
                v = outer[l * 4 + edge_rows[y]] if y in edge_rows else inner[l * (rows - 4) + y - 2]
                m = jnp.sum(v, axis=0, keepdims=True) / members
                mean = jnp.where(sub == y, m, mean)
                a = v - m
                hi = a.astype(BF16)
                to = (q, pl.ds(y * members, members), pl.ds(h * width, width))
                hi_ref[to] = hi
                lo_ref[to] = (a - hi.astype(F32)).astype(BF16)
            centre_ref[pl.ds(pl.multiple_of(l * rows, rows), rows), :] = mean
        pltpu.make_async_copy(lo_ref.at[q], lo_hbm.at[q], sem.at[q]).start()
        return carry

    def finish(q, carry):
        pltpu.make_async_copy(lo_ref.at[q], lo_hbm.at[q], sem.at[q]).wait()
        return carry

    lax.fori_loop(0, levels // 2, pair, 0)
    lax.fori_loop(0, levels // 2, finish, 0)


def anomalies(dims, inner, outer):
    members, levels, rows, width = dims
    shape = (levels // 2, rows * members, 2 * width)
    return pl.pallas_call(
        functools.partial(spread_kernel, dims),
        name="anomalies",
        out_shape=(VMEM(shape, BF16), pltpu.HBM(shape, BF16), VMEM((levels * rows, width), F32)),
        in_specs=[IN_VMEM] * 2,
        out_specs=[IN_VMEM, IN_HBM, IN_VMEM],
        scratch_shapes=[VMEM(shape, BF16), pltpu.SemaphoreType.DMA((levels // 2,))],
        **grant(8, 8_000_000, 8_000_000),
    )(*near(inner, outer))


def moments_kernel(members, blocks_dev, block, n_parts, devices, *refs):
    parts, (obs_ref, var_ref, _, prior_ref, innov_ref, packed_ref) = refs[:n_parts], refs[n_parts:]
    scaled, both = [], []
    for b in range(blocks_dev):
        at = pl.ds(b * members, members)
        total = parts[0][at, :]
        for part in parts[1:]:
            total = total + part[at, :]
        prior_ref[:, pl.ds(b * block, block)] = total
        mean = jnp.sum(total, axis=0, keepdims=True) / members
        dev = total - mean
        var = var_ref[pl.ds(b, 1), :]
        misfit = obs_ref[pl.ds(b, 1), :] - mean
        innov_ref[pl.ds(b, 1), :] = misfit / jnp.sqrt(var)
        scaled.append(dev / var)
        both.append(jnp.concatenate([dev, jnp.broadcast_to(misfit, (SUB, block))], axis=0))
    left = jnp.concatenate(scaled, axis=1)
    right = jnp.concatenate(both, axis=1)
    g = lax.dot_general(left, right, (((1,), (1,)), ((), ())), precision=lax.Precision.HIGHEST,
                        preferred_element_type=F32)
    wide = jnp.concatenate([g, jnp.zeros((members, 128 - g.shape[1]), F32)], axis=1)
    lane = lanes_of((SUB, 128))
    packed = jnp.zeros((SUB, 128), F32)
    groups = members // SUB
    start = 0
    for i in range(groups):
        v = wide[i * SUB:(i + 1) * SUB]
        stop = start + SUB * (i + 1)
        moved = pltpu.roll(v, start, 1) if start else v
        packed = jnp.where((lane >= start) & (lane < stop), moved, packed)
        start = stop
    for i in range(groups):
        v = wide[i * SUB:(i + 1) * SUB]
        packed = jnp.where(lane == start + i, pltpu.roll(v, start + i - members, 1), packed)
    for device in range(devices):
        packed_ref[pl.ds(device * SUB, SUB), :] = packed


def moments(parts, obs, var, after, members, blocks_dev, block, devices):
    return pl.pallas_call(
        functools.partial(moments_kernel, members, blocks_dev, block, len(parts), devices),
        name="moments",
        out_shape=(jax.ShapeDtypeStruct((members, blocks_dev * block), F32),
                   jax.ShapeDtypeStruct((blocks_dev, block), F32),
                   VMEM((devices * SUB, 128), F32)),
        in_specs=[IN_VMEM] * (len(parts) + 3),
        out_specs=[IN_VMEM] * 3,
        **grant(8, 4_000_000, 400_000),
    )(*near(*parts), obs, var, *near(after))


def weights(gathered, members, devices):
    groups = members // SUB
    lane = lanes_of((SUB, 128))
    sub = subs_of((SUB, 128))
    total = gathered[pl.ds(0, SUB), :]
    for d in range(1, devices):
        total = total + gathered[pl.ds(d * SUB, SUB), :]
    lower, start = [], 0
    for i in range(groups):
        v = pltpu.roll(total, (128 - start) % 128, 1) if start else total
        lower.append(jnp.where(lane < SUB * (i + 1), v, 0.0))
        start += SUB * (i + 1)
    upper = jnp.transpose(jnp.concatenate(lower, axis=0))
    upper = upper[:members]
    upper = jnp.concatenate([upper, jnp.zeros((members, 128 - members), F32)], axis=1)
    rows = []
    for i in range(groups):
        a = jnp.where(lane < SUB * (i + 1), lower[i], upper[i * SUB:(i + 1) * SUB])
        a = jnp.where(lane < members, a, 0.0)
        a = a + jnp.where(lane == sub + SUB * i, members - 1.0, 0.0)
        a = jnp.where(lane == members + sub + SUB * i, 1.0, a)
        pull = pltpu.roll(total, (2 * members - start - i) % 128, 1)
        rows.append(jnp.where(lane == 2 * members, pull, a))
    for k in range(members):
        i0, s = divmod(k, SUB)
        pivot_row = jnp.broadcast_to(rows[i0][s:s + 1, :], (SUB, 128))
        pivot = jnp.broadcast_to(pivot_row[:, k:k + 1], (SUB, 128))
        ratio = pivot_row / pivot
        for i in range(i0, groups):
            if i == i0 and s == SUB - 1:
                continue
            factor = jnp.broadcast_to(rows[i][:, k:k + 1], (SUB, 128))
            if i == i0:
                factor = jnp.where(sub > s, factor, 0.0)
            rows[i] = rows[i] - factor * ratio
    mean_weight = jnp.zeros((SUB, 128), F32)
    for i in range(groups):
        pivot = jnp.sum(jnp.where(lane == sub + SUB * i, rows[i], 0.0), axis=1, keepdims=True)
        rows[i] = rows[i] / jnp.sqrt(pivot)
        mean_weight = mean_weight + rows[i] * rows[i][:, 2 * members:2 * members + 1]
    mean_weight = jnp.sum(mean_weight, axis=0, keepdims=True)
    return [mean_weight + math.sqrt(members - 1.0) * r for r in rows]


def update_kernel(dims, devices, gathered, hi_ref, centre_ref, lo_hbm, out_hbm, mat_hi, mat_lo, done, lo_ref, sem, lo_sem):
    members, levels, rows, width = dims
    fetch = pltpu.make_async_copy(lo_hbm, lo_ref, lo_sem)
    fetch.start()
    size = rows * members
    lane = lanes_of((rows, 128))
    sub = subs_of((rows, 128))
    copies = 128 // members
    made = weights(gathered, members, devices)
    for i, r in enumerate(made):
        r = jnp.where(lane < members, pltpu.roll(r, 128 - members, 1), 0.0)
        tiled = r
        for q in range(1, copies):
            tiled = tiled + pltpu.roll(r, q * members, 1)
        for s in range(0, SUB, 2):
            b = i * SUB + s
            for h in range(size // 128):
                keep = (lane // members) + h * copies == sub
                two = [jnp.where(keep, jnp.broadcast_to(tiled[t:t + 1], (rows, 128)), 0.0) for t in (s, s + 1)]
                m = jnp.concatenate(two, axis=0)
                big = m.astype(BF16)
                to = (pl.ds(b * rows, 2 * rows), pl.ds(h * 128, 128))
                mat_hi[to] = big
                mat_lo[to] = (m - big.astype(F32)).astype(BF16)

    fetch.wait()

    def copy(q):
        part = pl.ds(q * 2, 2)
        return pltpu.make_async_copy(done.at[:, part], out_hbm.at[:, part], sem.at[q])

    def pair(q, carry):
        dot = functools.partial(jnp.dot, preferred_element_type=F32)
        hi = hi_ref[q]
        acc = dot(mat_hi[...], hi) + dot(mat_hi[...], lo_ref[q]) + dot(mat_lo[...], hi)
        for h in range(2):
            l = q * 2 + h
            centre = centre_ref[pl.ds(pl.multiple_of(l * rows, rows), rows), :]
            done[:, l] = acc[:, h * width:(h + 1) * width].reshape(members, rows, width) + centre[None]
        copy(q).start()
        return carry

    lax.fori_loop(0, levels // 2, pair, 0)

    def finish(q, carry):
        copy(q).wait()
        return carry

    lax.fori_loop(0, levels // 2, finish, 0)


def update(gathered, hi, lo, centre, dims, devices):
    members, levels, rows, _ = dims
    return pl.pallas_call(
        functools.partial(update_kernel, dims, devices),
        name="update",
        out_shape=jax.ShapeDtypeStruct(dims, F32),
        in_specs=[IN_VMEM] * 3 + [IN_HBM],
        out_specs=IN_HBM,
        scratch_shapes=[VMEM((rows * members, rows * members), BF16)] * 2
        + [VMEM(dims, F32), VMEM(lo.shape, BF16), pltpu.SemaphoreType.DMA((levels // 2,)), pltpu.SemaphoreType.DMA],
        **grant(12, 2_000_000_000, 8_000_000),
    )(*near(gathered, hi, centre), *far(lo))


def per_device(sample_deviations, east_courant, north_courant, production, loss_rate, entry_count, entry_row,
               entry_block, path_weight, observed, obs_var):
    dims = members, levels, rows, width = sample_deviations.shape
    lat_size, lon_size = lax.axis_size("lat"), lax.axis_size("lon")
    block = path_weight.shape[2]
    blocks_dev = observed.shape[0] // block
    step = width // levels
    ring = lambda n, s: [(i, (i + s) % n) for i in range(n)]
    up = [(i, i + 1) for i in range(lat_size - 1)]
    down = [(j, i) for i, j in up]

    fields = (east_courant, north_courant, production, loss_rate)
    state, to_north, to_south, edge, local = pack(sample_deviations, fields)
    west = lax.ppermute(edge, "lon", ring(lon_size, 1))
    east = lax.ppermute(edge, "lon", ring(lon_size, lon_size - 1))
    below = lax.ppermute(to_north, "lat", up)
    above = lax.ppermute(to_south, "lat", down)
    from_west = ((jnp.arange(width) + 2) % step < 2)[None, :]
    top = slice((rows - 1) * members, rows * members)
    corner_s = lax.ppermute(jnp.where(from_west, west[top], east[top]), "lat", up)
    corner_n = lax.ppermute(jnp.where(from_west, west[:members], east[:members]), "lat", down)

    inner, *inside = interior(dims, state, local, edge, west, east, path_weight)
    outer, *sums = boundary(dims, state, inside, corner_s, corner_n, below, above,
                            entry_block, entry_row, entry_count, lat_size, blocks_dev)
    got = [sums[0]] + [lax.ppermute(sums[s], "lat", ring(lat_size, s)) for s in range(1, lat_size)]
    hi, lo, centre = anomalies(dims, inner, outer)
    devices = lat_size * lon_size
    prior, innovation, packed = moments(got, observed.reshape(blocks_dev, block), obs_var.reshape(blocks_dev, block),
                                        centre, members, blocks_dev, block, devices)
    gathered = lax.all_to_all(packed, ("lon", "lat"), 0, 0, tiled=True)
    updated = update(gathered, hi, lo, centre, dims, devices)
    return updated, prior, innovation.reshape(observed.shape)


def solution(mesh):
    tile = P(None, "lat", "lon")
    owned = P(("lon", "lat"))
    in_specs = (P(None, None, "lat", "lon"), tile, tile, tile, tile, owned, owned, owned,
                P(("lon", "lat"), None, None), owned, owned)
    out_specs = (P(None, None, "lat", "lon"), P(None, ("lon", "lat")), owned)
    return jax.shard_map(per_device, mesh=mesh, in_specs=in_specs, out_specs=out_specs, check_vma=False)
```

```python
import functools
import math

import jax
import jax.numpy as jnp
from jax import lax
from jax.experimental import pallas as pl
from jax.experimental.pallas import tpu as pltpu
from jax.sharding import PartitionSpec as P


SUB = 8
F32 = jnp.float32
BF16 = jnp.bfloat16
VMEM = pltpu.VMEM
SMEM = pltpu.SMEM


def lanes_of(shape):
    return lax.broadcasted_iota(jnp.int32, shape, 1)


def subs_of(shape):
    return lax.broadcasted_iota(jnp.int32, shape, 0)


def grant(mib, flops, moved):
    return dict(
        compiler_params=pltpu.CompilerParams(vmem_limit_bytes=mib * 1024 * 1024),
        cost_estimate=pl.CostEstimate(flops=flops, bytes_accessed=moved, transcendentals=0),
    )


def near(*arrays):
    return [pltpu.with_memory_space_constraint(a, pltpu.VMEM) for a in arrays]


def far(*arrays):
    return [pltpu.with_memory_space_constraint(a, pltpu.HBM) for a in arrays]


IN_VMEM = pl.BlockSpec(memory_space=VMEM)
IN_SMEM = pl.BlockSpec(memory_space=SMEM)
IN_HBM = pl.BlockSpec(memory_space=pltpu.HBM)


def west_lanes(width, step):
    return ((lanes_of((SUB, width)) + 2) % step) < 2


def pack_kernel(dims, chunks, x_hbm, e_hbm, n_hbm, p_hbm, d_hbm, state, north, south, edge, to_east, to_west,
                fields, in_sem, field_sem):
    members, levels, rows, width = dims
    per = levels // chunks
    step = width // levels
    field_refs = (e_hbm, n_hbm, p_hbm, d_hbm)
    state_rows = 2 * levels * members

    def load(l, y):
        return pltpu.make_async_copy(x_hbm.at[:, l, y], state.at[l * rows + y], in_sem.at[l // per])

    def load_field(f):
        return pltpu.make_async_copy(field_refs[f], fields.at[f], field_sem.at[f])

    for f in range(4):
        load_field(f).start()
    for l in range(levels):
        for y in range(rows):
            load(l, y).start()
    lane = lanes_of((SUB, width))
    level_of = ((lane + 2) // step) % levels
    edge[...] = jnp.zeros_like(edge)
    for f in range(4):
        load_field(f).wait()
        acc = jnp.zeros((SUB, width), F32)
        for l in range(levels):
            acc = jnp.where(level_of == l, pltpu.roll(fields[f, l], (step * l) % width, 1), acc)
        edge[pl.ds(rows * members + f * rows, rows), :] = acc
        for l in range(levels):
            at = pl.ds(state_rows + l * 4 + f, 1)
            north[at, :] = fields[f, l, rows - 1:rows]
            south[at, :] = fields[f, l, 0:1]
    for c in range(chunks):
        first = c * per
        for l in range(first, first + per):
            for y in range(rows):
                load(l, y).wait()
        for l in range(first, first + per):
            for r in range(2):
                at = pl.ds((l * 2 + r) * members, members)
                south[at, :] = state[l * rows + r]
                north[at, :] = state[l * rows + rows - 2 + r]
        for y in range(rows):
            for g in range(members // SUB):
                at = pl.ds(y * members + g * SUB, SUB)
                acc = edge[at, :]
                for l in range(first, first + per):
                    v = state[l * rows + y, pl.ds(g * SUB, SUB), :]
                    acc = jnp.where(level_of == l, pltpu.roll(v, (step * l) % width, 1), acc)
                edge[at, :] = acc
    from_west = west_lanes(width, step)
    tiles = [(y * members + g * SUB, (y + 1) * members + g * SUB, (y // 2) * members + g * SUB)
             for y in range(0, rows, 2) for g in range(members // SUB)]
    start = rows * members
    tiles += [(start + f * rows, start + (f + 1) * rows, start // 2 + (f // 2) * rows) for f in (0, 2)]
    for even, odd, to in tiles:
        a, b = edge[pl.ds(even, SUB), :], edge[pl.ds(odd, SUB), :]
        to_east[pl.ds(to, SUB), :] = jnp.where(from_west, a, pltpu.roll(b, width - 2, 1))
        to_west[pl.ds(to, SUB), :] = jnp.where(from_west, pltpu.roll(b, 2, 1), a)


def pack(x, fields, chunks=4):
    members, levels, rows, width = x.shape
    halo = 2 * levels * members + 4 * levels
    edge = rows * members + 4 * rows
    return pl.pallas_call(
        functools.partial(pack_kernel, x.shape, chunks),
        name="pack_halos",
        out_shape=(
            VMEM((levels * rows, members, width), F32),
            VMEM((halo, width), F32),
            VMEM((halo, width), F32),
            VMEM((edge, width), F32),
            VMEM((edge // 2, width), F32),
            VMEM((edge // 2, width), F32),
            VMEM((4, levels, rows, width), F32),
        ),
        in_specs=[IN_HBM] * 5,
        out_specs=[IN_VMEM] * 7,
        scratch_shapes=[
            pltpu.SemaphoreType.DMA((chunks,)),
            pltpu.SemaphoreType.DMA((4,)),
        ],
        **grant(8, 4_000_000, 8_000_000),
    )(*far(x, *fields))


def stencil(e, n, p, d):
    keep = 1.0 - d
    ep, em = jnp.maximum(e, 0.0), jnp.minimum(e, 0.0)
    np_, nm = jnp.maximum(n, 0.0), jnp.minimum(n, 0.0)
    return (
        keep * (1.0 - ep + em - np_ + nm),
        keep * ep,
        -(keep * em),
        keep * np_,
        -(keep * nm),
        p,
    )


def closed(c):
    lane = lanes_of(c[1].shape)
    width = c[1].shape[1]
    c0, cw, ce, cs, cn, p = c
    return c0, jnp.where(lane == 0, 0.0, cw), jnp.where(lane == width - 1, 0.0, ce), cs, cn, p


def advance(mid, low, high, c):
    c0, cw, ce, cs, cn, p = c
    out = []
    for g, v in enumerate(mid):
        total = (c0 * v + cw * pltpu.roll(v, 1, 1)) + (ce * pltpu.roll(v, v.shape[1] - 1, 1) + p)
        if low is not None:
            total = total + cs * low[g]
        if high is not None:
            total = total + cn * high[g]
        out.append(total)
    return out


def spread(tile, row):
    return jnp.broadcast_to(tile[row:row + 1], (SUB, tile.shape[1]))


def open_strip(packed, base, odd, back, width):
    tile = packed[pl.ds(base, SUB), :]
    return pltpu.roll(tile, back % width, 1) if odd else tile


def corners_kernel(dims, edge, west, east, first_out, last_out):
    members, levels, rows, width = dims
    from_west = west_lanes(width, width // levels)
    for g in range(members // SUB):
        at = pl.ds(g * SUB, SUB)
        base = (rows // 2 - 1) * members + g * SUB
        first_out[at, :] = jnp.where(from_west, west[at, :], east[at, :])
        last_out[at, :] = jnp.where(from_west, open_strip(west, base, True, 2, width),
                                    open_strip(east, base, True, -2, width))
    start = rows * members
    sub = subs_of((SUB, width))
    for out, y in ((first_out, 0), (last_out, rows - 1)):
        picked = jnp.zeros((SUB, width), F32)
        for f in range(4):
            picked = jnp.where(sub == f, spread(edge[pl.ds(start + f * rows, rows), :], y), picked)
        out[pl.ds(members, SUB), :] = picked


def corners(dims, edge, west, east):
    members, _, _, width = dims
    shape = (members + SUB, width)
    return pl.pallas_call(
        functools.partial(corners_kernel, dims),
        name="corners",
        out_shape=[VMEM(shape, F32)] * 2,
        in_specs=[IN_VMEM] * 3,
        out_specs=[IN_VMEM] * 2,
        **grant(8, 100_000, 400_000),
    )(*near(edge, west, east))


def columns_kernel(dims, edge, west, east, corner_s, corner_n, fix, fix_sum, halo, change, halo1):
    members, levels, rows, width = dims
    groups = members // SUB
    step = width // levels
    lane = lanes_of((SUB, width))
    kind = lane % step
    from_west = west_lanes(width, step)
    is_first, is_last = kind == 0, kind == step - 1
    start = rows * members
    outside = []
    for f in range(4):
        base = start // 2 + (f // 2) * rows
        outside.append(jnp.where(from_west, open_strip(west, base, f % 2, 2, width),
                                 open_strip(east, base, f % 2, -2, width)))
    outside = stencil(*outside)
    own = stencil(*[edge[pl.ds(start + f * rows, rows), :] for f in range(4)])

    def change_of(values, cw, ce):
        entering = jnp.where(is_first, cw * pltpu.roll(values, 1, 1), 0.0)
        return jnp.where(is_last, ce * pltpu.roll(values, width - 1, 1), entering)

    for y in range(-1, rows + 1):
        if y < 0 or y >= rows:
            source = corner_s if y < 0 else corner_n
            fields = source[pl.ds(members, SUB), :]
            c = stencil(*[spread(fields, f) for f in range(4)])
            cw, ce = c[1], c[2]
        else:
            cw, ce = spread(own[1], y), spread(own[2], y)
        for g in range(groups):
            at = pl.ds((y + 1) * members + g * SUB, SUB)
            if y < 0 or y >= rows:
                values = source[pl.ds(g * SUB, SUB), :]
            else:
                base = (y // 2) * members + g * SUB
                values = jnp.where(from_west, open_strip(west, base, y % 2, 2, width),
                                   open_strip(east, base, y % 2, -2, width))
            halo[at, :] = values
            change[at, :] = change_of(values, cw, ce)
    for y in range(rows):
        c0, cw, ce, cs, cn, p = [spread(t, y) for t in outside]
        k0, kw, ke, ks, kn, _ = [spread(t, y) for t in own]
        for g in range(groups):
            at = pl.ds(y * members + g * SUB, SUB)
            low, mid, high = [pl.ds((y + d) * members + g * SUB, SUB) for d in range(3)]
            base = (y // 2) * members + g * SUB
            inner = edge[at, :]
            aw = open_strip(west, base, y % 2, 2, width)
            ae = open_strip(east, base, y % 2, -2, width)
            side_w = jnp.where(from_west, pltpu.roll(aw, 1, 1), pltpu.roll(inner, 1, 1))
            side_e = jnp.where(from_west, pltpu.roll(inner, width - 1, 1), pltpu.roll(ae, width - 1, 1))
            beyond = (c0 * halo[mid, :] + cw * side_w) + (ce * side_e + cs * halo[low, :]) + (cn * halo[high, :] + p)
            moved = change[mid, :]
            total = k0 * moved + ks * change[low, :] + kn * change[high, :] + change_of(beyond, kw, ke)
            total = jnp.where(kind == 1, kw * pltpu.roll(moved, 1, 1), total)
            total = jnp.where(kind == 2, ke * pltpu.roll(moved, width - 1, 1), total)
            fix[at, :] = total
            shift = step
            while shift < width:
                total = total + pltpu.roll(total, shift, 1)
                shift *= 2
            fix_sum[at, :] = jnp.where((lane < 2) | (lane >= width - 2), total, 0.0)


def columns(dims, edge, west, east, corner_s, corner_n):
    members, levels, rows, width = dims
    if width != 4 * levels:
        raise ValueError("strip width")
    shape = (rows * members, width)
    return pl.pallas_call(
        functools.partial(columns_kernel, dims),
        name="columns",
        out_shape=[VMEM(shape, F32)] * 2,
        in_specs=[IN_VMEM] * 5,
        out_specs=[IN_VMEM] * 2,
        scratch_shapes=[VMEM(((rows + 2) * members, width), F32)] * 2 + [VMEM(shape, F32)],
        **grant(8, 2_000_000, 1_000_000),
    )(*near(edge, west, east, corner_s, corner_n))


def interior_kernel(dims, state, fields, pw_hbm, inner, part, content, coef, pw, pw_sem):
    members, levels, rows, _ = dims
    groups = members // SUB
    fetch = pltpu.make_async_copy(pw_hbm, pw, pw_sem)
    fetch.start()
    content[...] = jnp.zeros_like(content)

    def level(l, carry):
        base = pl.multiple_of(l * rows, rows)
        got = closed(stencil(*[fields[f, l] for f in range(4)]))
        for k, c in enumerate(got):
            coef[l, k] = c

        def load(ref, row):
            return [ref[row, pl.ds(g * SUB, SUB), :] for g in range(groups)]

        def store(ref, row, values):
            for g in range(groups):
                ref[row, pl.ds(g * SUB, SUB), :] = values[g]

        before, now = None, load(state, base)
        older, old, older_c = None, None, None
        for y in range(rows):
            after = load(state, base + y + 1) if y < rows - 1 else None
            c = [spread(t, y) for t in got]
            new = advance(now, before, after, c)
            if y in (0, 1, rows - 2, rows - 1):
                store(part, l * 6 + {0: 0, 1: 1, rows - 2: 2, rows - 1: 3}[y], new)
            y2 = y - 1
            if y2 >= 1:
                done = advance(old, older if y2 > 1 else None, new if y2 < rows - 2 else None, older_c)
                if y2 == 1:
                    store(part, l * 6 + 4, done)
                elif y2 == rows - 2:
                    store(part, l * 6 + 5, done)
                else:
                    store(inner, l * (rows - 4) + y2 - 2, done)
                    for g in range(groups):
                        content[pl.ds((y2 - 2) * members + g * SUB, SUB), :] += done[g]
            older, old, older_c = old, new, c
            before, now = now, after
        return carry

    lax.fori_loop(0, levels, level, 0)
    fetch.wait()


def interior(dims, state, fields, pw):
    members, levels, rows, width = dims
    shapes = (
        (levels * (rows - 4), members, width),
        (levels * 6, members, width),
        ((rows - 4) * members, width),
        (levels, 6, rows, width),
    )
    return pl.pallas_call(
        functools.partial(interior_kernel, dims),
        name="interior",
        out_shape=[VMEM(s, F32) for s in shapes] + [VMEM(pw.shape, BF16)],
        in_specs=[IN_VMEM] * 2 + [IN_HBM],
        out_specs=[IN_VMEM] * 5,
        scratch_shapes=[pltpu.SemaphoreType.DMA],
        **grant(8, 60_000_000, 12_000_000),
    )(*near(state, fields), *far(pw))


def boundary_kernel(dims, lat_size, slots, blocks_dev, block_of, row_of, count,
                    state, part, inner_content, coef, pw, fix_sum, below, above, outer, *rest):
    members, levels, rows, _ = dims
    outs, (content, content16, rays) = rest[:lat_size], rest[lat_size:]
    groups = members // SUB
    tail = 2 * levels * members
    edge_rows = (0, 1, rows - 2, rows - 1)
    for y in edge_rows:
        at = pl.ds(y * members, members)
        content[at, :] = fix_sum[at, :]
    middle = pl.ds(2 * members, (rows - 4) * members)
    content[middle, :] = inner_content[...] + fix_sum[middle, :]

    def level(l, half):
        base = pl.multiple_of(l * rows, rows)

        def halo_row(ref, r):
            start = pl.multiple_of((l * 2 + r) * members, members)
            return [ref[pl.ds(start + g * SUB, SUB), :] for g in range(groups)]

        def halo_coefs(ref):
            values = ref[pl.ds(pl.multiple_of(tail + (l - half) * 4, SUB), SUB), :]
            return closed(stencil(*[spread(values, half * 4 + f) for f in range(4)]))

        def load(ref, row):
            return [ref[row, pl.ds(g * SUB, SUB), :] for g in range(groups)]

        def add(partial, c, values):
            return [q + c * v for q, v in zip(partial, values)]

        south1, north1 = halo_row(below, 1), halo_row(above, 0)
        lower = advance(south1, halo_row(below, 0), load(state, base), halo_coefs(below))
        upper = advance(north1, load(state, base + rows - 1), halo_row(above, 1), halo_coefs(above))
        tiles = [coef[l, k] for k in range(6)]
        c_first = [spread(t, 0) for t in tiles]
        c_last = [spread(t, rows - 1) for t in tiles]
        first = add(load(part, l * 6), c_first[3], south1)
        last = add(load(part, l * 6 + 3), c_last[4], north1)
        done = (
            advance(first, lower, load(part, l * 6 + 1), c_first),
            add(load(part, l * 6 + 4), spread(tiles[3], 1), first),
            add(load(part, l * 6 + 5), spread(tiles[4], rows - 2), last),
            advance(last, load(part, l * 6 + 2), upper, c_last),
        )
        for i, y in enumerate(edge_rows):
            for g in range(groups):
                content[pl.ds(y * members + g * SUB, SUB), :] += done[i][g]
                outer[l * 4 + i, pl.ds(g * SUB, SUB), :] = done[i][g]

    def two_levels(q, carry):
        for half in range(2):
            level(q * 2 + half, half)
        return carry

    lax.fori_loop(0, levels // 2, two_levels, 0)
    content16[...] = (content[...] / math.sqrt(levels)).astype(BF16)
    rays[...] = jnp.zeros_like(rays)
    live = count[0]
    mine = lax.axis_index("lat")
    for k in range(slots):
        picked = content16[pl.ds(pl.multiple_of(row_of[k] * members, members), members), :]
        partial = jnp.dot(picked, pw[k], preferred_element_type=F32)
        partial = jnp.where(k < live, partial, 0.0)
        place = block_of[k] - mine * blocks_dev
        place = jnp.where(place < 0, place + lat_size * blocks_dev, place)
        at = pl.ds(pl.multiple_of(place * members, members), members)
        rays[at, :] += partial
    size = blocks_dev * members
    for s in range(lat_size):
        outs[s][...] = rays[pl.ds(s * size, size), :]


def boundary(dims, state, inside, fix_sum, below, above, block_of, row_of, count, lat_size, blocks_dev):
    members, levels, rows, width = dims
    slots, _, block = inside[-1].shape
    size = blocks_dev * members
    return pl.pallas_call(
        functools.partial(boundary_kernel, dims, lat_size, slots, blocks_dev),
        name="boundary_rays",
        out_shape=[VMEM((levels * 4, members, width), F32)] + [VMEM((size, block), F32)] * lat_size,
        in_specs=[IN_SMEM] * 3 + [IN_VMEM] * 8,
        out_specs=[IN_VMEM] * (1 + lat_size),
        scratch_shapes=[
            VMEM((rows * members, width), F32),
            VMEM((rows * members, width), BF16),
            VMEM((lat_size * size, block), F32),
        ],
        **grant(8, 30_000_000, 12_000_000),
    )(block_of, row_of, count, *near(state, *inside, fix_sum, below, above))


def spread_kernel(dims, inner, outer, fix, hi_ref, lo_hbm, centre_ref, lo_ref, sem):
    members, levels, rows, width = dims
    sub = subs_of((rows, width))
    lane = lanes_of((members, width))
    near_edge = (lane < 2) | (lane >= width - 2)
    edge_rows = {0: 0, 1: 1, rows - 2: 2, rows - 1: 3}

    def pair(q, carry):
        for h in range(2):
            l = q * 2 + h
            mean = jnp.zeros((rows, width), F32)
            for y in range(rows):
                v = outer[l * 4 + edge_rows[y]] if y in edge_rows else inner[l * (rows - 4) + y - 2]
                turned = pltpu.roll(fix[pl.ds(y * members, members), :], (width - (width // levels) * l) % width, 1)
                v = v + jnp.where(near_edge, turned, 0.0)
                m = jnp.sum(v, axis=0, keepdims=True) / members
                mean = jnp.where(sub == y, m, mean)
                a = v - m
                hi = a.astype(BF16)
                to = (q, pl.ds(y * members, members), pl.ds(h * width, width))
                hi_ref[to] = hi
                lo_ref[to] = (a - hi.astype(F32)).astype(BF16)
            centre_ref[pl.ds(pl.multiple_of(l * rows, rows), rows), :] = mean
        pltpu.make_async_copy(lo_ref.at[q], lo_hbm.at[q], sem.at[q]).start()
        return carry

    def finish(q, carry):
        pltpu.make_async_copy(lo_ref.at[q], lo_hbm.at[q], sem.at[q]).wait()
        return carry

    lax.fori_loop(0, levels // 2, pair, 0)
    lax.fori_loop(0, levels // 2, finish, 0)


def anomalies(dims, inner, outer, fix):
    members, levels, rows, width = dims
    shape = (levels // 2, rows * members, 2 * width)
    return pl.pallas_call(
        functools.partial(spread_kernel, dims),
        name="anomalies",
        out_shape=(VMEM(shape, BF16), pltpu.HBM(shape, BF16), VMEM((levels * rows, width), F32)),
        in_specs=[IN_VMEM] * 3,
        out_specs=[IN_VMEM, IN_HBM, IN_VMEM],
        scratch_shapes=[VMEM(shape, BF16), pltpu.SemaphoreType.DMA((levels // 2,))],
        **grant(8, 8_000_000, 8_000_000),
    )(*near(inner, outer, fix))


def moments_kernel(members, blocks_dev, block, n_parts, devices, *refs):
    parts, (obs_ref, var_ref, _, prior_ref, innov_ref, packed_ref) = refs[:n_parts], refs[n_parts:]
    scaled, both = [], []
    for b in range(blocks_dev):
        at = pl.ds(b * members, members)
        total = parts[0][at, :]
        for part in parts[1:]:
            total = total + part[at, :]
        prior_ref[:, pl.ds(b * block, block)] = total
        mean = jnp.sum(total, axis=0, keepdims=True) / members
        dev = total - mean
        var = var_ref[pl.ds(b, 1), :]
        misfit = obs_ref[pl.ds(b, 1), :] - mean
        innov_ref[pl.ds(b, 1), :] = misfit / jnp.sqrt(var)
        scaled.append(dev / var)
        both.append(jnp.concatenate([dev, jnp.broadcast_to(misfit, (SUB, block))], axis=0))
    left = jnp.concatenate(scaled, axis=1)
    right = jnp.concatenate(both, axis=1)
    g = lax.dot_general(left, right, (((1,), (1,)), ((), ())), precision=lax.Precision.HIGHEST,
                        preferred_element_type=F32)
    wide = jnp.concatenate([g, jnp.zeros((members, 128 - g.shape[1]), F32)], axis=1)
    lane = lanes_of((SUB, 128))
    packed = jnp.zeros((SUB, 128), F32)
    groups = members // SUB
    start = 0
    for i in range(groups):
        v = wide[i * SUB:(i + 1) * SUB]
        stop = start + SUB * (i + 1)
        moved = pltpu.roll(v, start, 1) if start else v
        packed = jnp.where((lane >= start) & (lane < stop), moved, packed)
        start = stop
    for i in range(groups):
        v = wide[i * SUB:(i + 1) * SUB]
        packed = jnp.where(lane == start + i, pltpu.roll(v, start + i - members, 1), packed)
    for device in range(devices):
        packed_ref[pl.ds(device * SUB, SUB), :] = packed


def moments(parts, obs, var, after, members, blocks_dev, block, devices):
    return pl.pallas_call(
        functools.partial(moments_kernel, members, blocks_dev, block, len(parts), devices),
        name="moments",
        out_shape=(jax.ShapeDtypeStruct((members, blocks_dev * block), F32),
                   jax.ShapeDtypeStruct((blocks_dev, block), F32),
                   VMEM((devices * SUB, 128), F32)),
        in_specs=[IN_VMEM] * (len(parts) + 3),
        out_specs=[IN_VMEM] * 3,
        **grant(8, 4_000_000, 400_000),
    )(*near(*parts), obs, var, *near(after))


def weights(gathered, members, devices):
    groups = members // SUB
    lane = lanes_of((SUB, 128))
    sub = subs_of((SUB, 128))
    total = gathered[pl.ds(0, SUB), :]
    for d in range(1, devices):
        total = total + gathered[pl.ds(d * SUB, SUB), :]
    lower, start = [], 0
    for i in range(groups):
        v = pltpu.roll(total, (128 - start) % 128, 1) if start else total
        lower.append(jnp.where(lane < SUB * (i + 1), v, 0.0))
        start += SUB * (i + 1)
    upper = jnp.transpose(jnp.concatenate(lower, axis=0))
    upper = upper[:members]
    upper = jnp.concatenate([upper, jnp.zeros((members, 128 - members), F32)], axis=1)
    rows = []
    for i in range(groups):
        a = jnp.where(lane < SUB * (i + 1), lower[i], upper[i * SUB:(i + 1) * SUB])
        a = jnp.where(lane < members, a, 0.0)
        a = a + jnp.where(lane == sub + SUB * i, members - 1.0, 0.0)
        a = jnp.where(lane == members + sub + SUB * i, 1.0, a)
        pull = pltpu.roll(total, (2 * members - start - i) % 128, 1)
        rows.append(jnp.where(lane == 2 * members, pull, a))
    for k in range(members):
        i0, s = divmod(k, SUB)
        pivot_row = jnp.broadcast_to(rows[i0][s:s + 1, :], (SUB, 128))
        pivot = jnp.broadcast_to(pivot_row[:, k:k + 1], (SUB, 128))
        ratio = pivot_row / pivot
        for i in range(i0, groups):
            if i == i0 and s == SUB - 1:
                continue
            factor = jnp.broadcast_to(rows[i][:, k:k + 1], (SUB, 128))
            if i == i0:
                factor = jnp.where(sub > s, factor, 0.0)
            rows[i] = rows[i] - factor * ratio
    mean_weight = jnp.zeros((SUB, 128), F32)
    for i in range(groups):
        pivot = jnp.sum(jnp.where(lane == sub + SUB * i, rows[i], 0.0), axis=1, keepdims=True)
        rows[i] = rows[i] / jnp.sqrt(pivot)
        mean_weight = mean_weight + rows[i] * rows[i][:, 2 * members:2 * members + 1]
    mean_weight = jnp.sum(mean_weight, axis=0, keepdims=True)
    return [mean_weight + math.sqrt(members - 1.0) * r for r in rows]


def update_kernel(dims, devices, gathered, hi_ref, centre_ref, lo_hbm, out_hbm, mat_hi, mat_lo, done, lo_ref, sem, lo_sem):
    members, levels, rows, width = dims
    fetch = pltpu.make_async_copy(lo_hbm, lo_ref, lo_sem)
    fetch.start()
    size = rows * members
    lane = lanes_of((rows, 128))
    sub = subs_of((rows, 128))
    copies = 128 // members
    made = weights(gathered, members, devices)
    for i, r in enumerate(made):
        r = jnp.where(lane < members, pltpu.roll(r, 128 - members, 1), 0.0)
        tiled = r
        for q in range(1, copies):
            tiled = tiled + pltpu.roll(r, q * members, 1)
        for s in range(0, SUB, 2):
            b = i * SUB + s
            for h in range(size // 128):
                keep = (lane // members) + h * copies == sub
                two = [jnp.where(keep, jnp.broadcast_to(tiled[t:t + 1], (rows, 128)), 0.0) for t in (s, s + 1)]
                m = jnp.concatenate(two, axis=0)
                big = m.astype(BF16)
                to = (pl.ds(b * rows, 2 * rows), pl.ds(h * 128, 128))
                mat_hi[to] = big
                mat_lo[to] = (m - big.astype(F32)).astype(BF16)

    fetch.wait()

    def copy(q):
        part = pl.ds(q * 2, 2)
        return pltpu.make_async_copy(done.at[:, part], out_hbm.at[:, part], sem.at[q])

    def pair(q, carry):
        dot = functools.partial(jnp.dot, preferred_element_type=F32)
        hi = hi_ref[q]
        acc = dot(mat_hi[...], hi) + dot(mat_hi[...], lo_ref[q]) + dot(mat_lo[...], hi)
        for h in range(2):
            l = q * 2 + h
            centre = centre_ref[pl.ds(pl.multiple_of(l * rows, rows), rows), :]
            done[:, l] = acc[:, h * width:(h + 1) * width].reshape(members, rows, width) + centre[None]
        copy(q).start()
        return carry

    lax.fori_loop(0, levels // 2, pair, 0)

    def finish(q, carry):
        copy(q).wait()
        return carry

    lax.fori_loop(0, levels // 2, finish, 0)


def update(gathered, hi, lo, centre, dims, devices):
    members, levels, rows, _ = dims
    return pl.pallas_call(
        functools.partial(update_kernel, dims, devices),
        name="update",
        out_shape=jax.ShapeDtypeStruct(dims, F32),
        in_specs=[IN_VMEM] * 3 + [IN_HBM],
        out_specs=IN_HBM,
        scratch_shapes=[VMEM((rows * members, rows * members), BF16)] * 2
        + [VMEM(dims, F32), VMEM(lo.shape, BF16), pltpu.SemaphoreType.DMA((levels // 2,)), pltpu.SemaphoreType.DMA],
        **grant(12, 2_000_000_000, 8_000_000),
    )(*near(gathered, hi, centre), *far(lo))


def per_device(sample_deviations, east_courant, north_courant, production, loss_rate, entry_count, entry_row,
               entry_block, path_weight, observed, obs_var):
    dims = members, levels, rows, width = sample_deviations.shape
    lat_size, lon_size = lax.axis_size("lat"), lax.axis_size("lon")
    block = path_weight.shape[2]
    blocks_dev = observed.shape[0] // block
    ring = lambda n, s: [(i, (i + s) % n) for i in range(n)]
    up = [(i, i + 1) for i in range(lat_size - 1)]
    down = [(j, i) for i, j in up]

    fields = (east_courant, north_courant, production, loss_rate)
    state, to_north, to_south, edge, to_east, to_west, local = pack(sample_deviations, fields)
    west = lax.ppermute(to_east, "lon", ring(lon_size, 1))
    east = lax.ppermute(to_west, "lon", ring(lon_size, lon_size - 1))
    below = lax.ppermute(to_north, "lat", up)
    above = lax.ppermute(to_south, "lat", down)
    inner, *inside = interior(dims, state, local, path_weight)
    first, last = corners(dims, edge, west, east)
    corner_s = lax.ppermute(last, "lat", up)
    corner_n = lax.ppermute(first, "lat", down)
    fix, fix_sum = columns(dims, edge, west, east, corner_s, corner_n)
    outer, *sums = boundary(dims, state, inside, fix_sum, below, above,
                            entry_block, entry_row, entry_count, lat_size, blocks_dev)
    got = [sums[0]] + [lax.ppermute(sums[s], "lat", ring(lat_size, s)) for s in range(1, lat_size)]
    hi, lo, centre = anomalies(dims, inner, outer, fix)
    devices = lat_size * lon_size
    prior, innovation, packed = moments(got, observed.reshape(blocks_dev, block), obs_var.reshape(blocks_dev, block),
                                        centre, members, blocks_dev, block, devices)
    gathered = lax.all_to_all(packed, ("lon", "lat"), 0, 0, tiled=True)
    updated = update(gathered, hi, lo, centre, dims, devices)
    return updated, prior, innovation.reshape(observed.shape)


def solution(mesh):
    tile = P(None, "lat", "lon")
    owned = P(("lon", "lat"))
    in_specs = (P(None, None, "lat", "lon"), tile, tile, tile, tile, owned, owned, owned,
                P(("lon", "lat"), None, None), owned, owned)
    out_specs = (P(None, None, "lat", "lon"), P(None, ("lon", "lat")), owned)
    return jax.shard_map(per_device, mesh=mesh, in_specs=in_specs, out_specs=out_specs, check_vma=False)
```

```python
import functools
import math

import jax
import jax.numpy as jnp
from jax import lax
from jax.experimental import pallas as pl
from jax.experimental.pallas import tpu as pltpu
from jax.sharding import PartitionSpec as P


SUB = 8
F32 = jnp.float32
BF16 = jnp.bfloat16
VMEM = pltpu.VMEM
SMEM = pltpu.SMEM


def lanes_of(shape):
    return lax.broadcasted_iota(jnp.int32, shape, 1)


def subs_of(shape):
    return lax.broadcasted_iota(jnp.int32, shape, 0)


def grant(mib, flops, moved):
    return dict(
        compiler_params=pltpu.CompilerParams(vmem_limit_bytes=mib * 1024 * 1024),
        cost_estimate=pl.CostEstimate(flops=flops, bytes_accessed=moved, transcendentals=0),
    )


def near(*arrays):
    return [pltpu.with_memory_space_constraint(a, pltpu.VMEM) for a in arrays]


def far(*arrays):
    return [pltpu.with_memory_space_constraint(a, pltpu.HBM) for a in arrays]


IN_VMEM = pl.BlockSpec(memory_space=VMEM)
IN_SMEM = pl.BlockSpec(memory_space=SMEM)
IN_HBM = pl.BlockSpec(memory_space=pltpu.HBM)


def west_lanes(width, step):
    return ((lanes_of((SUB, width)) + 2) % step) < 2


def pack_kernel(dims, chunks, x_hbm, e_hbm, n_hbm, p_hbm, d_hbm, state, north, south, edge, to_east, to_west,
                fields, in_sem, field_sem):
    members, levels, rows, width = dims
    per = levels // chunks
    step = width // levels
    field_refs = (e_hbm, n_hbm, p_hbm, d_hbm)
    state_rows = 2 * levels * members

    def load(l, y):
        return pltpu.make_async_copy(x_hbm.at[:, l, y], state.at[l * rows + y], in_sem.at[l // per])

    def load_field(f):
        return pltpu.make_async_copy(field_refs[f], fields.at[f], field_sem.at[f])

    for f in range(4):
        load_field(f).start()
    for l in range(levels):
        for y in range(rows):
            load(l, y).start()
    lane = lanes_of((SUB, width))
    level_of = ((lane + 2) // step) % levels
    edge[...] = jnp.zeros_like(edge)
    for f in range(4):
        load_field(f).wait()
        acc = jnp.zeros((SUB, width), F32)
        for l in range(levels):
            acc = jnp.where(level_of == l, pltpu.roll(fields[f, l], (step * l) % width, 1), acc)
        edge[pl.ds(rows * members + f * rows, rows), :] = acc
        for l in range(levels):
            at = pl.ds(state_rows + l * 4 + f, 1)
            north[at, :] = fields[f, l, rows - 1:rows]
            south[at, :] = fields[f, l, 0:1]
    for c in range(chunks):
        first = c * per
        for l in range(first, first + per):
            for y in range(rows):
                load(l, y).wait()
        for l in range(first, first + per):
            for r in range(2):
                at = pl.ds((l * 2 + r) * members, members)
                south[at, :] = state[l * rows + r]
                north[at, :] = state[l * rows + rows - 2 + r]
        for y in range(rows):
            for g in range(members // SUB):
                at = pl.ds(y * members + g * SUB, SUB)
                acc = edge[at, :]
                for l in range(first, first + per):
                    v = state[l * rows + y, pl.ds(g * SUB, SUB), :]
                    acc = jnp.where(level_of == l, pltpu.roll(v, (step * l) % width, 1), acc)
                edge[at, :] = acc
    from_west = west_lanes(width, step)
    tiles = [(y * members + g * SUB, (y + 1) * members + g * SUB, (y // 2) * members + g * SUB)
             for y in range(0, rows, 2) for g in range(members // SUB)]
    start = rows * members
    tiles += [(start + f * rows, start + (f + 1) * rows, start // 2 + (f // 2) * rows) for f in (0, 2)]
    for even, odd, to in tiles:
        a, b = edge[pl.ds(even, SUB), :], edge[pl.ds(odd, SUB), :]
        to_east[pl.ds(to, SUB), :] = jnp.where(from_west, a, pltpu.roll(b, width - 2, 1))
        to_west[pl.ds(to, SUB), :] = jnp.where(from_west, pltpu.roll(b, 2, 1), a)


def pack(x, fields, chunks=4):
    members, levels, rows, width = x.shape
    halo = 2 * levels * members + 4 * levels
    edge = rows * members + 4 * rows
    return pl.pallas_call(
        functools.partial(pack_kernel, x.shape, chunks),
        name="pack_halos",
        out_shape=(
            VMEM((levels * rows, members, width), F32),
            VMEM((halo, width), F32),
            VMEM((halo, width), F32),
            VMEM((edge, width), F32),
            VMEM((edge // 2, width), F32),
            VMEM((edge // 2, width), F32),
            VMEM((4, levels, rows, width), F32),
        ),
        in_specs=[IN_HBM] * 5,
        out_specs=[IN_VMEM] * 7,
        scratch_shapes=[
            pltpu.SemaphoreType.DMA((chunks,)),
            pltpu.SemaphoreType.DMA((4,)),
        ],
        **grant(8, 4_000_000, 8_000_000),
    )(*far(x, *fields))


def stencil(e, n, p, d):
    keep = 1.0 - d
    ep, em = jnp.maximum(e, 0.0), jnp.minimum(e, 0.0)
    np_, nm = jnp.maximum(n, 0.0), jnp.minimum(n, 0.0)
    return (
        keep * (1.0 - ep + em - np_ + nm),
        keep * ep,
        -(keep * em),
        keep * np_,
        -(keep * nm),
        p,
    )


def closed(c):
    lane = lanes_of(c[1].shape)
    width = c[1].shape[1]
    c0, cw, ce, cs, cn, p = c
    return c0, jnp.where(lane == 0, 0.0, cw), jnp.where(lane == width - 1, 0.0, ce), cs, cn, p


def advance(mid, low, high, c):
    c0, cw, ce, cs, cn, p = c
    out = []
    for g, v in enumerate(mid):
        total = (c0 * v + cw * pltpu.roll(v, 1, 1)) + (ce * pltpu.roll(v, v.shape[1] - 1, 1) + p)
        if low is not None:
            total = total + cs * low[g]
        if high is not None:
            total = total + cn * high[g]
        out.append(total)
    return out


def spread(tile, row):
    return jnp.broadcast_to(tile[row:row + 1], (SUB, tile.shape[1]))


def open_strip(packed, base, odd, back, width):
    tile = packed[pl.ds(base, SUB), :]
    return pltpu.roll(tile, back % width, 1) if odd else tile


def corners_kernel(dims, edge, west, east, first_out, last_out):
    members, levels, rows, width = dims
    from_west = west_lanes(width, width // levels)
    for g in range(members // SUB):
        at = pl.ds(g * SUB, SUB)
        base = (rows // 2 - 1) * members + g * SUB
        first_out[at, :] = jnp.where(from_west, west[at, :], east[at, :])
        last_out[at, :] = jnp.where(from_west, open_strip(west, base, True, 2, width),
                                    open_strip(east, base, True, -2, width))
    start = rows * members
    sub = subs_of((SUB, width))
    for out, y in ((first_out, 0), (last_out, rows - 1)):
        picked = jnp.zeros((SUB, width), F32)
        for f in range(4):
            picked = jnp.where(sub == f, spread(edge[pl.ds(start + f * rows, rows), :], y), picked)
        out[pl.ds(members, SUB), :] = picked


def corners(dims, edge, west, east):
    members, _, _, width = dims
    shape = (members + SUB, width)
    return pl.pallas_call(
        functools.partial(corners_kernel, dims),
        name="corners",
        out_shape=[VMEM(shape, F32)] * 2,
        in_specs=[IN_VMEM] * 3,
        out_specs=[IN_VMEM] * 2,
        **grant(8, 100_000, 400_000),
    )(*near(edge, west, east))


def change_of(values, cw, ce, step):
    width = values.shape[1]
    kind = lanes_of(values.shape) % step
    entering = jnp.where(kind == 0, cw * pltpu.roll(values, 1, 1), 0.0)
    return jnp.where(kind == step - 1, ce * pltpu.roll(values, width - 1, 1), entering)


def level_sums(tiles, step):
    width = tiles[0].shape[1]
    lane = lanes_of(tiles[0].shape)
    shift = step
    while shift < width:
        tiles = [t + pltpu.roll(t, shift, 1) for t in tiles]
        shift *= 2
    return [jnp.where((lane < 2) | (lane >= width - 2), t, 0.0) for t in tiles]


def columns_kernel(dims, edge, west, east, fix, fix_sum, side):
    members, levels, rows, width = dims
    groups = members // SUB
    step = width // levels
    kind = lanes_of((SUB, width)) % step
    from_west = west_lanes(width, step)
    start = rows * members
    outside = []
    for f in range(4):
        base = start // 2 + (f // 2) * rows
        outside.append(jnp.where(from_west, open_strip(west, base, f % 2, 2, width),
                                 open_strip(east, base, f % 2, -2, width)))
    outside = stencil(*outside)
    own = stencil(*[edge[pl.ds(start + f * rows, rows), :] for f in range(4)])
    all_tiles = []
    for g in range(groups):
        halo, change, side_w, side_e = [], [], [], []
        for y in range(rows):
            base = (y // 2) * members + g * SUB
            aw = open_strip(west, base, y % 2, 2, width)
            ae = open_strip(east, base, y % 2, -2, width)
            inner = edge[pl.ds(y * members + g * SUB, SUB), :]
            halo.append(jnp.where(from_west, aw, ae))
            change.append(change_of(halo[-1], spread(own[1], y), spread(own[2], y), step))
            side_w.append(pltpu.roll(jnp.where(kind == step - 1, inner, aw), 1, 1))
            side_e.append(pltpu.roll(jnp.where(kind == 0, inner, ae), width - 1, 1))
        for y in range(rows):
            c0, cw, ce, cs, cn, p = [spread(t, y) for t in outside]
            k0, kw, ke, ks, kn, _ = [spread(t, y) for t in own]
            beyond = (c0 * halo[y] + cw * side_w[y]) + (ce * side_e[y] + p)
            total = k0 * change[y]
            if y > 0:
                beyond = beyond + cs * halo[y - 1]
                total = total + ks * change[y - 1]
            if y < rows - 1:
                beyond = beyond + cn * halo[y + 1]
                total = total + kn * change[y + 1]
            total = total + change_of(beyond, kw, ke, step)
            total = jnp.where(kind == 1, kw * pltpu.roll(change[y], 1, 1), total)
            total = jnp.where(kind == 2, ke * pltpu.roll(change[y], width - 1, 1), total)
            all_tiles.append(total)
    at = 0
    for y, own_side, far_side in ((0, own[3], outside[3]), (rows - 1, own[4], outside[4])):
        for t in (own_side, own[1], own[2], far_side):
            side[at] = spread(t, y)
            at += 1
    sums = level_sums(all_tiles, step)
    for g in range(groups):
        for y in range(rows):
            to = pl.ds(y * members + g * SUB, SUB)
            fix[to, :] = all_tiles[g * rows + y]
            fix_sum[to, :] = sums[g * rows + y]


def columns(dims, edge, west, east):
    members, levels, rows, width = dims
    if width != 4 * levels:
        raise ValueError("strip width")
    shape = (rows * members, width)
    return pl.pallas_call(
        functools.partial(columns_kernel, dims),
        name="columns",
        out_shape=[VMEM(shape, F32)] * 2 + [VMEM((8, SUB, width), F32)],
        in_specs=[IN_VMEM] * 3,
        out_specs=[IN_VMEM] * 3,
        **grant(8, 2_000_000, 1_000_000),
    )(*near(edge, west, east))


def interior_kernel(dims, state, fields, pw_hbm, inner, part, content, coef, pw, pw_sem):
    members, levels, rows, _ = dims
    groups = members // SUB
    fetch = pltpu.make_async_copy(pw_hbm, pw, pw_sem)
    fetch.start()
    content[...] = jnp.zeros_like(content)

    def level(l, carry):
        base = pl.multiple_of(l * rows, rows)
        got = closed(stencil(*[fields[f, l] for f in range(4)]))
        for k, c in enumerate(got):
            coef[l, k] = c

        def load(ref, row):
            return [ref[row, pl.ds(g * SUB, SUB), :] for g in range(groups)]

        def store(ref, row, values):
            for g in range(groups):
                ref[row, pl.ds(g * SUB, SUB), :] = values[g]

        before, now = None, load(state, base)
        older, old, older_c = None, None, None
        for y in range(rows):
            after = load(state, base + y + 1) if y < rows - 1 else None
            c = [spread(t, y) for t in got]
            new = advance(now, before, after, c)
            if y in (0, 1, rows - 2, rows - 1):
                store(part, l * 6 + {0: 0, 1: 1, rows - 2: 2, rows - 1: 3}[y], new)
            y2 = y - 1
            if y2 >= 1:
                done = advance(old, older if y2 > 1 else None, new if y2 < rows - 2 else None, older_c)
                if y2 == 1:
                    store(part, l * 6 + 4, done)
                elif y2 == rows - 2:
                    store(part, l * 6 + 5, done)
                else:
                    store(inner, l * (rows - 4) + y2 - 2, done)
                    for g in range(groups):
                        content[pl.ds((y2 - 2) * members + g * SUB, SUB), :] += done[g]
            older, old, older_c = old, new, c
            before, now = now, after
        return carry

    lax.fori_loop(0, levels, level, 0)
    fetch.wait()


def interior(dims, state, fields, pw):
    members, levels, rows, width = dims
    shapes = (
        (levels * (rows - 4), members, width),
        (levels * 6, members, width),
        ((rows - 4) * members, width),
        (levels, 6, rows, width),
    )
    return pl.pallas_call(
        functools.partial(interior_kernel, dims),
        name="interior",
        out_shape=[VMEM(s, F32) for s in shapes] + [VMEM(pw.shape, BF16)],
        in_specs=[IN_VMEM] * 2 + [IN_HBM],
        out_specs=[IN_VMEM] * 5,
        scratch_shapes=[pltpu.SemaphoreType.DMA],
        **grant(8, 60_000_000, 12_000_000),
    )(*near(state, fields), *far(pw))


def boundary_kernel(dims, lat_size, slots, blocks_dev, block_of, row_of, count,
                    state, part, inner_content, coef, pw, fix, fix_sum, side, corner_s, corner_n, below, above,
                    outer_hbm, fix_ends, *rest):
    members, levels, rows, width = dims
    outs, (content, content16, rays, outer, outer_sem) = rest[:lat_size], rest[lat_size:]
    groups = members // SUB
    tail = 2 * levels * members
    edge_rows = (0, 1, rows - 2, rows - 1)
    step = width // levels
    extras = []
    for i, (y, corner) in enumerate(((0, corner_s), (rows - 1, corner_n))):
        fields = corner[pl.ds(members, SUB), :]
        c = stencil(*[spread(fields, f) for f in range(4)])
        ks, kw, ke, cs = [side[4 * i + d] for d in range(4)]
        for g in range(groups):
            values = corner[pl.ds(g * SUB, SUB), :]
            extra = ks * change_of(values, c[1], c[2], step) + change_of(cs * values, kw, ke, step)
            extras.append((i, y, g, extra))
    sums = level_sums([e[-1] for e in extras], step)
    for (i, y, g, extra), total in zip(extras, sums):
        at = pl.ds(y * members + g * SUB, SUB)
        fix_ends[pl.ds(i * members + g * SUB, SUB), :] = fix[at, :] + extra
        content[at, :] = fix_sum[at, :] + total
    for y in (1, rows - 2):
        at = pl.ds(y * members, members)
        content[at, :] = fix_sum[at, :]
    middle = pl.ds(2 * members, (rows - 4) * members)
    content[middle, :] = inner_content[...] + fix_sum[middle, :]

    def level(l, half):
        base = pl.multiple_of(l * rows, rows)

        def halo_row(ref, r):
            start = pl.multiple_of((l * 2 + r) * members, members)
            return [ref[pl.ds(start + g * SUB, SUB), :] for g in range(groups)]

        def halo_coefs(ref):
            values = ref[pl.ds(pl.multiple_of(tail + (l - half) * 4, SUB), SUB), :]
            return closed(stencil(*[spread(values, half * 4 + f) for f in range(4)]))

        def load(ref, row):
            return [ref[row, pl.ds(g * SUB, SUB), :] for g in range(groups)]

        def add(partial, c, values):
            return [q + c * v for q, v in zip(partial, values)]

        south1, north1 = halo_row(below, 1), halo_row(above, 0)
        lower = advance(south1, halo_row(below, 0), load(state, base), halo_coefs(below))
        upper = advance(north1, load(state, base + rows - 1), halo_row(above, 1), halo_coefs(above))
        tiles = [coef[l, k] for k in range(6)]
        c_first = [spread(t, 0) for t in tiles]
        c_last = [spread(t, rows - 1) for t in tiles]
        first = add(load(part, l * 6), c_first[3], south1)
        last = add(load(part, l * 6 + 3), c_last[4], north1)
        done = (
            advance(first, lower, load(part, l * 6 + 1), c_first),
            add(load(part, l * 6 + 4), spread(tiles[3], 1), first),
            add(load(part, l * 6 + 5), spread(tiles[4], rows - 2), last),
            advance(last, load(part, l * 6 + 2), upper, c_last),
        )
        for i, y in enumerate(edge_rows):
            for g in range(groups):
                content[pl.ds(y * members + g * SUB, SUB), :] += done[i][g]
                outer[l * 4 + i, pl.ds(g * SUB, SUB), :] = done[i][g]

    def put(q):
        part = pl.ds(q * 8, 8)
        return pltpu.make_async_copy(outer.at[part], outer_hbm.at[part], outer_sem.at[q])

    def two_levels(q, carry):
        for half in range(2):
            level(q * 2 + half, half)
        put(q).start()
        return carry

    lax.fori_loop(0, levels // 2, two_levels, 0)
    content16[...] = (content[...] / math.sqrt(levels)).astype(BF16)
    rays[...] = jnp.zeros_like(rays)
    live = count[0]
    mine = lax.axis_index("lat")
    for k in range(slots):
        picked = content16[pl.ds(pl.multiple_of(row_of[k] * members, members), members), :]
        partial = jnp.dot(picked, pw[k], preferred_element_type=F32)
        partial = jnp.where(k < live, partial, 0.0)
        place = block_of[k] - mine * blocks_dev
        place = jnp.where(place < 0, place + lat_size * blocks_dev, place)
        at = pl.ds(pl.multiple_of(place * members, members), members)
        rays[at, :] += partial
    size = blocks_dev * members
    for s in range(lat_size):
        outs[s][...] = rays[pl.ds(s * size, size), :]
    for q in range(levels // 2):
        put(q).wait()


def boundary(dims, state, inside, sides, corner_s, corner_n, below, above, block_of, row_of, count, lat_size, blocks_dev):
    members, levels, rows, width = dims
    slots, _, block = inside[-1].shape
    size = blocks_dev * members
    return pl.pallas_call(
        functools.partial(boundary_kernel, dims, lat_size, slots, blocks_dev),
        name="boundary_rays",
        out_shape=[pltpu.HBM((levels * 4, members, width), F32), VMEM((2 * members, width), F32)]
        + [VMEM((size, block), F32)] * lat_size,
        in_specs=[IN_SMEM] * 3 + [IN_VMEM] * 12,
        out_specs=[IN_HBM] + [IN_VMEM] * (1 + lat_size),
        scratch_shapes=[
            VMEM((rows * members, width), F32),
            VMEM((rows * members, width), BF16),
            VMEM((lat_size * size, block), F32),
            VMEM((levels * 4, members, width), F32),
            pltpu.SemaphoreType.DMA((levels // 2,)),
        ],
        **grant(8, 30_000_000, 12_000_000),
    )(block_of, row_of, count, *near(state, *inside, *sides, corner_s, corner_n, below, above))


def spread_kernel(dims, inner, fix, fix_ends, outer_hbm, hi_hbm, lo_hbm, centre_ref,
                  outer, hi_ref, lo_ref, outer_sem, hi_sem, lo_sem):
    members, levels, rows, width = dims
    sub = subs_of((rows, width))
    lane = lanes_of((members, width))
    near_edge = (lane < 2) | (lane >= width - 2)
    edge_rows = {0: 0, 1: 1, rows - 2: 2, rows - 1: 3}

    def get(q):
        part = pl.ds(q * 8, 8)
        return pltpu.make_async_copy(outer_hbm.at[part], outer.at[part], outer_sem.at[q])

    def put_hi(q):
        return pltpu.make_async_copy(hi_ref.at[q], hi_hbm.at[q], hi_sem.at[q])

    def put_lo(q):
        return pltpu.make_async_copy(lo_ref.at[q], lo_hbm.at[q], lo_sem.at[q])

    def begin(q, carry):
        get(q).start()
        return carry

    def pair(q, carry):
        get(q).wait()
        for h in range(2):
            l = q * 2 + h
            turn = (width - (width // levels) * l) % width
            mean = jnp.zeros((rows, width), F32)
            for y in range(rows):
                v = outer[l * 4 + edge_rows[y]] if y in edge_rows else inner[l * (rows - 4) + y - 2]
                if y in (0, rows - 1):
                    add = fix_ends[pl.ds((0 if y == 0 else 1) * members, members), :]
                else:
                    add = fix[pl.ds(y * members, members), :]
                v = v + jnp.where(near_edge, pltpu.roll(add, turn, 1), 0.0)
                m = jnp.sum(v, axis=0, keepdims=True) / members
                mean = jnp.where(sub == y, m, mean)
                a = v - m
                hi = a.astype(BF16)
                to = (q, pl.ds(y * members, members), pl.ds(h * width, width))
                hi_ref[to] = hi
                lo_ref[to] = (a - hi.astype(F32)).astype(BF16)
            centre_ref[pl.ds(pl.multiple_of(l * rows, rows), rows), :] = mean
        put_hi(q).start()
        put_lo(q).start()
        return carry

    def finish(q, carry):
        put_hi(q).wait()
        put_lo(q).wait()
        return carry

    lax.fori_loop(0, levels // 2, begin, 0)
    lax.fori_loop(0, levels // 2, pair, 0)
    lax.fori_loop(0, levels // 2, finish, 0)


def anomalies(dims, inner, outer, fix, fix_ends):
    members, levels, rows, width = dims
    shape = (levels // 2, rows * members, 2 * width)
    return pl.pallas_call(
        functools.partial(spread_kernel, dims),
        name="anomalies",
        out_shape=(pltpu.HBM(shape, BF16), pltpu.HBM(shape, BF16), VMEM((levels * rows, width), F32)),
        in_specs=[IN_VMEM] * 3 + [IN_HBM],
        out_specs=[IN_HBM] * 2 + [IN_VMEM],
        scratch_shapes=[VMEM(outer.shape, F32), VMEM(shape, BF16), VMEM(shape, BF16)]
        + [pltpu.SemaphoreType.DMA((levels // 2,))] * 3,
        **grant(12, 8_000_000, 8_000_000),
    )(*near(inner, fix, fix_ends), *far(outer))


def moments_kernel(members, blocks_dev, block, n_parts, devices, *refs):
    parts, (obs_ref, var_ref, prior_ref, innov_ref, packed_ref) = refs[:n_parts], refs[n_parts:]
    scaled, both = [], []
    for b in range(blocks_dev):
        at = pl.ds(b * members, members)
        total = parts[0][at, :]
        for part in parts[1:]:
            total = total + part[at, :]
        prior_ref[:, pl.ds(b * block, block)] = total
        mean = jnp.sum(total, axis=0, keepdims=True) / members
        dev = total - mean
        var = var_ref[pl.ds(b, 1), :]
        misfit = obs_ref[pl.ds(b, 1), :] - mean
        innov_ref[pl.ds(b, 1), :] = misfit / jnp.sqrt(var)
        scaled.append(dev / var)
        both.append(jnp.concatenate([dev, jnp.broadcast_to(misfit, (SUB, block))], axis=0))
    left = jnp.concatenate(scaled, axis=1)
    right = jnp.concatenate(both, axis=1)
    g = lax.dot_general(left, right, (((1,), (1,)), ((), ())), precision=lax.Precision.HIGHEST,
                        preferred_element_type=F32)
    wide = jnp.concatenate([g, jnp.zeros((members, 128 - g.shape[1]), F32)], axis=1)
    lane = lanes_of((SUB, 128))
    packed = jnp.zeros((SUB, 128), F32)
    groups = members // SUB
    start = 0
    for i in range(groups):
        v = wide[i * SUB:(i + 1) * SUB]
        stop = start + SUB * (i + 1)
        moved = pltpu.roll(v, start, 1) if start else v
        packed = jnp.where((lane >= start) & (lane < stop), moved, packed)
        start = stop
    for i in range(groups):
        v = wide[i * SUB:(i + 1) * SUB]
        packed = jnp.where(lane == start + i, pltpu.roll(v, start + i - members, 1), packed)
    for device in range(devices):
        packed_ref[pl.ds(device * SUB, SUB), :] = packed


def moments(parts, obs, var, members, blocks_dev, block, devices):
    return pl.pallas_call(
        functools.partial(moments_kernel, members, blocks_dev, block, len(parts), devices),
        name="moments",
        out_shape=(jax.ShapeDtypeStruct((members, blocks_dev * block), F32),
                   jax.ShapeDtypeStruct((blocks_dev, block), F32),
                   VMEM((devices * SUB, 128), F32)),
        in_specs=[IN_VMEM] * (len(parts) + 2),
        out_specs=[IN_VMEM] * 3,
        **grant(8, 4_000_000, 400_000),
    )(*near(*parts), obs, var)


def weights(gathered, members, devices):
    groups = members // SUB
    lane = lanes_of((SUB, 128))
    sub = subs_of((SUB, 128))
    total = gathered[pl.ds(0, SUB), :]
    for d in range(1, devices):
        total = total + gathered[pl.ds(d * SUB, SUB), :]
    lower, start = [], 0
    for i in range(groups):
        v = pltpu.roll(total, (128 - start) % 128, 1) if start else total
        lower.append(jnp.where(lane < SUB * (i + 1), v, 0.0))
        start += SUB * (i + 1)
    upper = jnp.transpose(jnp.concatenate(lower, axis=0))
    upper = upper[:members]
    upper = jnp.concatenate([upper, jnp.zeros((members, 128 - members), F32)], axis=1)
    rows = []
    for i in range(groups):
        a = jnp.where(lane < SUB * (i + 1), lower[i], upper[i * SUB:(i + 1) * SUB])
        a = jnp.where(lane < members, a, 0.0)
        a = a + jnp.where(lane == sub + SUB * i, members - 1.0, 0.0)
        a = jnp.where(lane == members + sub + SUB * i, 1.0, a)
        pull = pltpu.roll(total, (2 * members - start - i) % 128, 1)
        rows.append(jnp.where(lane == 2 * members, pull, a))
    for k in range(0, members, 2):
        i0, s = divmod(k, SUB)
        f0 = [jnp.broadcast_to(r[:, k:k + 1], (SUB, 128)) for r in rows]
        f1 = [jnp.broadcast_to(r[:, k + 1:k + 2], (SUB, 128)) for r in rows]
        row0, row1 = spread(rows[i0], s), spread(rows[i0], s + 1)
        a, b, d = spread(f0[i0], s), spread(f1[i0], s), spread(f1[i0], s + 1)
        inv = 1.0 / a
        slope = b * inv
        low = row1 - slope * row0
        ratio0 = row0 * inv
        ratio1 = low * (1.0 / (d - slope * b))
        for i in range(i0, groups):
            g1 = f1[i] - slope * f0[i]
            change = f0[i] * ratio0
            second = g1 * ratio1
            if i == i0:
                change = jnp.where(sub > s, change, 0.0)
                second = jnp.where(sub > s + 1, second, 0.0)
            rows[i] = rows[i] - change - second
    mean_weight = jnp.zeros((SUB, 128), F32)
    for i in range(groups):
        pivot = jnp.sum(jnp.where(lane == sub + SUB * i, rows[i], 0.0), axis=1, keepdims=True)
        rows[i] = rows[i] / jnp.sqrt(pivot)
        mean_weight = mean_weight + rows[i] * rows[i][:, 2 * members:2 * members + 1]
    mean_weight = jnp.sum(mean_weight, axis=0, keepdims=True)
    return [mean_weight + math.sqrt(members - 1.0) * r for r in rows]


def update_kernel(dims, devices, gathered, centre_ref, hi_hbm, lo_hbm, out_hbm, mat_hi, mat_lo, done, hi_ref, lo_ref, sem, part_sem):
    members, levels, rows, width = dims
    half = levels // 4

    def get(source, target, part, k):
        at = pl.ds(part * half, half)
        return pltpu.make_async_copy(source.at[at], target.at[at], part_sem.at[k, part])

    for part in range(2):
        get(hi_hbm, hi_ref, part, 0).start()
        get(lo_hbm, lo_ref, part, 1).start()
    size = rows * members
    lane = lanes_of((rows, 128))
    sub = subs_of((rows, 128))
    copies = 128 // members
    made = weights(gathered, members, devices)
    for i, r in enumerate(made):
        r = jnp.where(lane < members, pltpu.roll(r, 128 - members, 1), 0.0)
        tiled = r
        for q in range(1, copies):
            tiled = tiled + pltpu.roll(r, q * members, 1)
        for s in range(0, SUB, 2):
            b = i * SUB + s
            for h in range(size // 128):
                keep = (lane // members) + h * copies == sub
                two = [jnp.where(keep, jnp.broadcast_to(tiled[t:t + 1], (rows, 128)), 0.0) for t in (s, s + 1)]
                m = jnp.concatenate(two, axis=0)
                big = m.astype(BF16)
                to = (pl.ds(b * rows, 2 * rows), pl.ds(h * 128, 128))
                mat_hi[to] = big
                mat_lo[to] = (m - big.astype(F32)).astype(BF16)

    def copy(q):
        part = pl.ds(q * 2, 2)
        return pltpu.make_async_copy(done.at[:, part], out_hbm.at[:, part], sem.at[q])

    def pair(q, carry):
        dot = functools.partial(jnp.dot, preferred_element_type=F32)
        hi = hi_ref[q]
        acc = dot(mat_hi[...], hi) + dot(mat_hi[...], lo_ref[q]) + dot(mat_lo[...], hi)
        for h in range(2):
            l = q * 2 + h
            centre = centre_ref[pl.ds(pl.multiple_of(l * rows, rows), rows), :]
            done[:, l] = acc[:, h * width:(h + 1) * width].reshape(members, rows, width) + centre[None]
        copy(q).start()
        return carry

    for part in range(2):
        get(hi_hbm, hi_ref, part, 0).wait()
        get(lo_hbm, lo_ref, part, 1).wait()
        lax.fori_loop(part * half, (part + 1) * half, pair, 0, unroll=4)

    def finish(q, carry):
        copy(q).wait()
        return carry

    lax.fori_loop(0, levels // 2, finish, 0)


def update(gathered, hi, lo, centre, dims, devices):
    members, levels, rows, _ = dims
    return pl.pallas_call(
        functools.partial(update_kernel, dims, devices),
        name="update",
        out_shape=jax.ShapeDtypeStruct(dims, F32),
        in_specs=[IN_VMEM] * 2 + [IN_HBM] * 2,
        out_specs=IN_HBM,
        scratch_shapes=[VMEM((rows * members, rows * members), BF16)] * 2
        + [VMEM(dims, F32), VMEM(lo.shape, BF16), VMEM(lo.shape, BF16), pltpu.SemaphoreType.DMA((levels // 2,)),
           pltpu.SemaphoreType.DMA((2, 2))],
        **grant(14, 2_000_000_000, 8_000_000),
    )(*near(gathered, centre), *far(hi, lo))


def per_device(sample_deviations, east_courant, north_courant, production, loss_rate, entry_count, entry_row,
               entry_block, path_weight, observed, obs_var):
    dims = members, levels, rows, width = sample_deviations.shape
    lat_size, lon_size = lax.axis_size("lat"), lax.axis_size("lon")
    block = path_weight.shape[2]
    blocks_dev = observed.shape[0] // block
    ring = lambda n, s: [(i, (i + s) % n) for i in range(n)]
    up = [(i, i + 1) for i in range(lat_size - 1)]
    down = [(j, i) for i, j in up]

    fields = (east_courant, north_courant, production, loss_rate)
    state, to_north, to_south, edge, to_east, to_west, local = pack(sample_deviations, fields)
    west = lax.ppermute(to_east, "lon", ring(lon_size, 1))
    east = lax.ppermute(to_west, "lon", ring(lon_size, lon_size - 1))
    below = lax.ppermute(to_north, "lat", up)
    above = lax.ppermute(to_south, "lat", down)
    inner, *inside = interior(dims, state, local, path_weight)
    first, last = corners(dims, edge, west, east)
    corner_s = lax.ppermute(last, "lat", up)
    corner_n = lax.ppermute(first, "lat", down)
    sides = columns(dims, edge, west, east)
    outer, fix_ends, *sums = boundary(dims, state, inside, sides, corner_s, corner_n, below, above,
                            entry_block, entry_row, entry_count, lat_size, blocks_dev)
    got = [sums[0]] + [lax.ppermute(sums[s], "lat", ring(lat_size, s)) for s in range(1, lat_size)]
    hi, lo, centre = anomalies(dims, inner, outer, sides[0], fix_ends)
    devices = lat_size * lon_size
    prior, innovation, packed = moments(got, observed.reshape(blocks_dev, block), obs_var.reshape(blocks_dev, block),
                                        members, blocks_dev, block, devices)
    gathered = lax.all_to_all(packed, ("lon", "lat"), 0, 0, tiled=True)
    updated = update(gathered, hi, lo, centre, dims, devices)
    return updated, prior, innovation.reshape(observed.shape)


def solution(mesh):
    tile = P(None, "lat", "lon")
    owned = P(("lon", "lat"))
    in_specs = (P(None, None, "lat", "lon"), tile, tile, tile, tile, owned, owned, owned,
                P(("lon", "lat"), None, None), owned, owned)
    out_specs = (P(None, None, "lat", "lon"), P(None, ("lon", "lat")), owned)
    return jax.shard_map(per_device, mesh=mesh, in_specs=in_specs, out_specs=out_specs, check_vma=False)
```

```python
import functools
import math

import jax
import jax.numpy as jnp
from jax import lax
from jax.experimental import pallas as pl
from jax.experimental.pallas import tpu as pltpu
from jax.sharding import PartitionSpec as P


SUB = 8
TOGETHER = 2
F32 = jnp.float32
BF16 = jnp.bfloat16
VMEM = pltpu.VMEM
SMEM = pltpu.SMEM


def lanes_of(shape):
    return lax.broadcasted_iota(jnp.int32, shape, 1)


def subs_of(shape):
    return lax.broadcasted_iota(jnp.int32, shape, 0)


def grant(mib, flops, moved):
    return dict(
        compiler_params=pltpu.CompilerParams(vmem_limit_bytes=mib * 1024 * 1024),
        cost_estimate=pl.CostEstimate(flops=flops, bytes_accessed=moved, transcendentals=0),
    )


def near(*arrays):
    return [pltpu.with_memory_space_constraint(a, pltpu.VMEM) for a in arrays]


def far(*arrays):
    return [pltpu.with_memory_space_constraint(a, pltpu.HBM) for a in arrays]


IN_VMEM = pl.BlockSpec(memory_space=VMEM)
IN_SMEM = pl.BlockSpec(memory_space=SMEM)
IN_HBM = pl.BlockSpec(memory_space=pltpu.HBM)


def west_lanes(width, step):
    return ((lanes_of((SUB, width)) + 2) % step) < 2


def pack_kernel(dims, chunks, x_hbm, e_hbm, n_hbm, p_hbm, d_hbm, state, north, south, edge, to_east, to_west,
                fields, in_sem, field_sem):
    members, levels, rows, width = dims
    per = levels // chunks
    step = width // levels
    field_refs = (e_hbm, n_hbm, p_hbm, d_hbm)
    state_rows = 2 * levels * members

    def load(l, y):
        return pltpu.make_async_copy(x_hbm.at[:, l, y], state.at[l * rows + y], in_sem.at[l // per])

    def load_field(f):
        return pltpu.make_async_copy(field_refs[f], fields.at[f], field_sem.at[f])

    for f in range(4):
        load_field(f).start()
    for l in range(levels):
        for y in range(rows):
            load(l, y).start()
    lane = lanes_of((SUB, width))
    level_of = ((lane + 2) // step) % levels
    edge[...] = jnp.zeros_like(edge)
    for f in range(4):
        load_field(f).wait()
        acc = jnp.zeros((SUB, width), F32)
        for l in range(levels):
            acc = jnp.where(level_of == l, pltpu.roll(fields[f, l], (step * l) % width, 1), acc)
        edge[pl.ds(rows * members + f * rows, rows), :] = acc
        for l in range(levels):
            at = pl.ds(state_rows + l * 4 + f, 1)
            north[at, :] = fields[f, l, rows - 1:rows]
            south[at, :] = fields[f, l, 0:1]
    for c in range(chunks):
        first = c * per
        for l in range(first, first + per):
            for y in range(rows):
                load(l, y).wait()
        for l in range(first, first + per):
            for r in range(2):
                at = pl.ds((l * 2 + r) * members, members)
                south[at, :] = state[l * rows + r]
                north[at, :] = state[l * rows + rows - 2 + r]
        for y in range(rows):
            for g in range(members // SUB):
                at = pl.ds(y * members + g * SUB, SUB)
                acc = edge[at, :]
                for l in range(first, first + per):
                    v = state[l * rows + y, pl.ds(g * SUB, SUB), :]
                    acc = jnp.where(level_of == l, pltpu.roll(v, (step * l) % width, 1), acc)
                edge[at, :] = acc
    from_west = west_lanes(width, step)
    tiles = [(y * members + g * SUB, (y + 1) * members + g * SUB, (y // 2) * members + g * SUB)
             for y in range(0, rows, 2) for g in range(members // SUB)]
    start = rows * members
    tiles += [(start + f * rows, start + (f + 1) * rows, start // 2 + (f // 2) * rows) for f in (0, 2)]
    for even, odd, to in tiles:
        a, b = edge[pl.ds(even, SUB), :], edge[pl.ds(odd, SUB), :]
        to_east[pl.ds(to, SUB), :] = jnp.where(from_west, a, pltpu.roll(b, width - 2, 1))
        to_west[pl.ds(to, SUB), :] = jnp.where(from_west, pltpu.roll(b, 2, 1), a)


def pack(x, fields, chunks=4):
    members, levels, rows, width = x.shape
    halo = 2 * levels * members + 4 * levels
    edge = rows * members + 4 * rows
    return pl.pallas_call(
        functools.partial(pack_kernel, x.shape, chunks),
        name="pack_halos",
        out_shape=(
            VMEM((levels * rows, members, width), F32),
            VMEM((halo, width), F32),
            VMEM((halo, width), F32),
            VMEM((edge, width), F32),
            VMEM((edge // 2, width), F32),
            VMEM((edge // 2, width), F32),
            VMEM((4, levels, rows, width), F32),
        ),
        in_specs=[IN_HBM] * 5,
        out_specs=[IN_VMEM] * 7,
        scratch_shapes=[
            pltpu.SemaphoreType.DMA((chunks,)),
            pltpu.SemaphoreType.DMA((4,)),
        ],
        **grant(8, 4_000_000, 8_000_000),
    )(*far(x, *fields))


def stencil(e, n, p, d):
    keep = 1.0 - d
    ep, em = jnp.maximum(e, 0.0), jnp.minimum(e, 0.0)
    np_, nm = jnp.maximum(n, 0.0), jnp.minimum(n, 0.0)
    return (
        keep * (1.0 - ep + em - np_ + nm),
        keep * ep,
        -(keep * em),
        keep * np_,
        -(keep * nm),
        p,
    )


def closed(c):
    lane = lanes_of(c[1].shape)
    width = c[1].shape[1]
    c0, cw, ce, cs, cn, p = c
    return c0, jnp.where(lane == 0, 0.0, cw), jnp.where(lane == width - 1, 0.0, ce), cs, cn, p


def advance(mid, low, high, c):
    c0, cw, ce, cs, cn, p = c
    out = []
    for g, v in enumerate(mid):
        total = (c0 * v + cw * pltpu.roll(v, 1, 1)) + (ce * pltpu.roll(v, v.shape[1] - 1, 1) + p)
        if low is not None:
            total = total + cs * low[g]
        if high is not None:
            total = total + cn * high[g]
        out.append(total)
    return out


def spread(tile, row):
    return jnp.broadcast_to(tile[row:row + 1], (SUB, tile.shape[1]))


def open_strip(packed, base, odd, back, width):
    tile = packed[pl.ds(base, SUB), :]
    return pltpu.roll(tile, back % width, 1) if odd else tile


def corners_kernel(dims, edge, west, east, first_out, last_out):
    members, levels, rows, width = dims
    from_west = west_lanes(width, width // levels)
    for g in range(members // SUB):
        at = pl.ds(g * SUB, SUB)
        base = (rows // 2 - 1) * members + g * SUB
        first_out[at, :] = jnp.where(from_west, west[at, :], east[at, :])
        last_out[at, :] = jnp.where(from_west, open_strip(west, base, True, 2, width),
                                    open_strip(east, base, True, -2, width))
    start = rows * members
    sub = subs_of((SUB, width))
    for out, y in ((first_out, 0), (last_out, rows - 1)):
        picked = jnp.zeros((SUB, width), F32)
        for f in range(4):
            picked = jnp.where(sub == f, spread(edge[pl.ds(start + f * rows, rows), :], y), picked)
        out[pl.ds(members, SUB), :] = picked


def corners(dims, edge, west, east):
    members, _, _, width = dims
    shape = (members + SUB, width)
    return pl.pallas_call(
        functools.partial(corners_kernel, dims),
        name="corners",
        out_shape=[VMEM(shape, F32)] * 2,
        in_specs=[IN_VMEM] * 3,
        out_specs=[IN_VMEM] * 2,
        **grant(8, 100_000, 400_000),
    )(*near(edge, west, east))


def change_of(values, cw, ce, step):
    width = values.shape[1]
    kind = lanes_of(values.shape) % step
    entering = jnp.where(kind == 0, cw * pltpu.roll(values, 1, 1), 0.0)
    return jnp.where(kind == step - 1, ce * pltpu.roll(values, width - 1, 1), entering)


def level_sums(tiles, step):
    width = tiles[0].shape[1]
    lane = lanes_of(tiles[0].shape)
    shift = step
    while shift < width:
        tiles = [t + pltpu.roll(t, shift, 1) for t in tiles]
        shift *= 2
    return [jnp.where((lane < 2) | (lane >= width - 2), t, 0.0) for t in tiles]


def columns_kernel(dims, edge, west, east, fix, fix_sum, side):
    members, levels, rows, width = dims
    groups = members // SUB
    step = width // levels
    kind = lanes_of((SUB, width)) % step
    from_west = west_lanes(width, step)
    start = rows * members
    outside = []
    for f in range(4):
        base = start // 2 + (f // 2) * rows
        outside.append(jnp.where(from_west, open_strip(west, base, f % 2, 2, width),
                                 open_strip(east, base, f % 2, -2, width)))
    outside = stencil(*outside)
    own = stencil(*[edge[pl.ds(start + f * rows, rows), :] for f in range(4)])
    all_tiles = []
    for g in range(groups):
        halo, change, side_w, side_e = [], [], [], []
        for y in range(rows):
            base = (y // 2) * members + g * SUB
            aw = open_strip(west, base, y % 2, 2, width)
            ae = open_strip(east, base, y % 2, -2, width)
            inner = edge[pl.ds(y * members + g * SUB, SUB), :]
            halo.append(jnp.where(from_west, aw, ae))
            change.append(change_of(halo[-1], spread(own[1], y), spread(own[2], y), step))
            side_w.append(pltpu.roll(jnp.where(kind == step - 1, inner, aw), 1, 1))
            side_e.append(pltpu.roll(jnp.where(kind == 0, inner, ae), width - 1, 1))
        for y in range(rows):
            c0, cw, ce, cs, cn, p = [spread(t, y) for t in outside]
            k0, kw, ke, ks, kn, _ = [spread(t, y) for t in own]
            beyond = (c0 * halo[y] + cw * side_w[y]) + (ce * side_e[y] + p)
            total = k0 * change[y]
            if y > 0:
                beyond = beyond + cs * halo[y - 1]
                total = total + ks * change[y - 1]
            if y < rows - 1:
                beyond = beyond + cn * halo[y + 1]
                total = total + kn * change[y + 1]
            total = total + change_of(beyond, kw, ke, step)
            total = jnp.where(kind == 1, kw * pltpu.roll(change[y], 1, 1), total)
            total = jnp.where(kind == 2, ke * pltpu.roll(change[y], width - 1, 1), total)
            all_tiles.append(total)
    at = 0
    for y, own_side, far_side in ((0, own[3], outside[3]), (rows - 1, own[4], outside[4])):
        for t in (own_side, own[1], own[2], far_side):
            side[at] = spread(t, y)
            at += 1
    sums = level_sums(all_tiles, step)
    for g in range(groups):
        for y in range(rows):
            to = pl.ds(y * members + g * SUB, SUB)
            fix[to, :] = all_tiles[g * rows + y]
            fix_sum[to, :] = sums[g * rows + y]


def columns(dims, edge, west, east):
    members, levels, rows, width = dims
    if width != 4 * levels:
        raise ValueError("strip width")
    shape = (rows * members, width)
    return pl.pallas_call(
        functools.partial(columns_kernel, dims),
        name="columns",
        out_shape=[VMEM(shape, F32)] * 2 + [VMEM((8, SUB, width), F32)],
        in_specs=[IN_VMEM] * 3,
        out_specs=[IN_VMEM] * 3,
        **grant(8, 2_000_000, 1_000_000),
    )(*near(edge, west, east))


def interior_kernel(dims, start, count, state, fields, *rest):
    members, _, rows, width = dims
    groups = members // SUB
    if len(rest) == 4:
        inner, part, content, coef = rest
        fetch = None
    else:
        pw_hbm, inner, part, content, coef, pw, pw_sem = rest
        fetch = pltpu.make_async_copy(pw_hbm, pw, pw_sem)
        fetch.start()

    def load(row):
        return [state[row, pl.ds(g * SUB, SUB), :] for g in range(groups)]

    def some_levels(q, sums):
        chosen = [q * TOGETHER + h for h in range(TOGETHER)]
        got = [closed(stencil(*[fields[f, start + l] for f in range(4)])) for l in chosen]
        before, now = [None] * TOGETHER, [load((start + l) * rows) for l in chosen]
        older, old, older_c = [None] * TOGETHER, [None] * TOGETHER, None
        sums = list(sums)
        for l, tiles in zip(chosen, got):
            for k, c in enumerate(tiles):
                coef[l, k] = c
        for y in range(rows):
            after = [load((start + l) * rows + y + 1) if y < rows - 1 else None for l in chosen]
            c = [[spread(t, y) for t in tiles] for tiles in got]
            new = [advance(now[h], before[h], after[h], c[h]) for h in range(TOGETHER)]
            y2 = y - 1
            done = None
            if y2 >= 1:
                done = [advance(old[h], older[h] if y2 > 1 else None, new[h] if y2 < rows - 2 else None, older_c[h])
                        for h in range(TOGETHER)]
            for h, l in enumerate(chosen):
                def store(ref, row, values):
                    for g in range(groups):
                        ref[row, pl.ds(g * SUB, SUB), :] = values[g]

                if y in (0, 1, rows - 2, rows - 1):
                    store(part, l * 6 + {0: 0, 1: 1, rows - 2: 2, rows - 1: 3}[y], new[h])
                if done is None:
                    continue
                if y2 == 1:
                    store(part, l * 6 + 4, done[h])
                elif y2 == rows - 2:
                    store(part, l * 6 + 5, done[h])
                else:
                    store(inner, l * (rows - 4) + y2 - 2, done[h])
                    sums[y2 - 2] = [t + d for t, d in zip(sums[y2 - 2], done[h])]
            older, old, older_c = old, new, c
            before, now = now, after
        return sums

    begin = [[jnp.zeros((SUB, width), F32)] * groups for _ in range(rows - 4)]
    sums = lax.fori_loop(0, count // TOGETHER, some_levels, begin)
    for y, row in enumerate(sums):
        for g in range(groups):
            content[pl.ds(y * members + g * SUB, SUB), :] = row[g]
    if fetch is not None:
        fetch.wait()


def interior(dims, start, count, state, fields, pw=None):
    members, _, rows, width = dims
    shapes = (
        (count * (rows - 4), members, width),
        (count * 6, members, width),
        ((rows - 4) * members, width),
        (count, 6, rows, width),
    )
    more = [] if pw is None else [pw]
    return pl.pallas_call(
        functools.partial(interior_kernel, dims, start, count),
        name="interior",
        out_shape=[VMEM(s, F32) for s in shapes] + [VMEM(m.shape, BF16) for m in more],
        in_specs=[IN_VMEM] * 2 + [IN_HBM] * len(more),
        out_specs=[IN_VMEM] * (4 + len(more)),
        scratch_shapes=[pltpu.SemaphoreType.DMA] * len(more),
        **grant(8, 30_000_000, 6_000_000),
    )(*near(state, fields), *far(*more))


def boundary_kernel(dims, lat_size, slots, blocks_dev, block_of, row_of, count,
                    state, part_a, content_a, coef_a, pw, part_b, content_b, coef_b, fix, fix_sum, side, corner_s, corner_n, below, above,
                    outer_hbm, fix_ends, *rest):
    members, levels, rows, width = dims
    outs, (content, content16, rays, outer, outer_sem) = rest[:lat_size], rest[lat_size:]
    groups = members // SUB
    tail = 2 * levels * members
    edge_rows = (0, 1, rows - 2, rows - 1)
    step = width // levels
    extras = []
    for i, (y, corner) in enumerate(((0, corner_s), (rows - 1, corner_n))):
        fields = corner[pl.ds(members, SUB), :]
        c = stencil(*[spread(fields, f) for f in range(4)])
        ks, kw, ke, cs = [side[4 * i + d] for d in range(4)]
        for g in range(groups):
            values = corner[pl.ds(g * SUB, SUB), :]
            extra = ks * change_of(values, c[1], c[2], step) + change_of(cs * values, kw, ke, step)
            extras.append((i, y, g, extra))
    sums = level_sums([e[-1] for e in extras], step)
    for (i, y, g, extra), total in zip(extras, sums):
        at = pl.ds(y * members + g * SUB, SUB)
        fix_ends[pl.ds(i * members + g * SUB, SUB), :] = fix[at, :] + extra
        content[at, :] = fix_sum[at, :] + total
    for y in (1, rows - 2):
        at = pl.ds(y * members, members)
        content[at, :] = fix_sum[at, :]
    middle = pl.ds(2 * members, (rows - 4) * members)
    content[middle, :] = content_a[...] + content_b[...] + fix_sum[middle, :]

    def level(l, half, part, coef, offset):
        here = l - offset
        base = pl.multiple_of(l * rows, rows)

        def halo_row(ref, r):
            start = pl.multiple_of((l * 2 + r) * members, members)
            return [ref[pl.ds(start + g * SUB, SUB), :] for g in range(groups)]

        def halo_coefs(ref):
            values = ref[pl.ds(pl.multiple_of(tail + (l - half) * 4, SUB), SUB), :]
            return closed(stencil(*[spread(values, half * 4 + f) for f in range(4)]))

        def load(ref, row):
            return [ref[row, pl.ds(g * SUB, SUB), :] for g in range(groups)]

        def add(partial, c, values):
            return [q + c * v for q, v in zip(partial, values)]

        south1, north1 = halo_row(below, 1), halo_row(above, 0)
        lower = advance(south1, halo_row(below, 0), load(state, base), halo_coefs(below))
        upper = advance(north1, load(state, base + rows - 1), halo_row(above, 1), halo_coefs(above))
        tiles = [coef[here, k] for k in range(6)]
        c_first = [spread(t, 0) for t in tiles]
        c_last = [spread(t, rows - 1) for t in tiles]
        first = add(load(part, here * 6), c_first[3], south1)
        last = add(load(part, here * 6 + 3), c_last[4], north1)
        done = (
            advance(first, lower, load(part, here * 6 + 1), c_first),
            add(load(part, here * 6 + 4), spread(tiles[3], 1), first),
            add(load(part, here * 6 + 5), spread(tiles[4], rows - 2), last),
            advance(last, load(part, here * 6 + 2), upper, c_last),
        )
        return done

    def put(q):
        part = pl.ds(q * 8, 8)
        return pltpu.make_async_copy(outer.at[part], outer_hbm.at[part], outer_sem.at[q])

    def two_levels(part, coef, offset, q, sums):
        both = [level(q * 2 + half, half, part, coef, offset) for half in range(2)]
        sums = [[t + a + b for t, a, b in zip(*row)] for row in zip(sums, *both)]
        for half, done in enumerate(both):
            for i in range(4):
                for g in range(groups):
                    outer[(q * 2 + half) * 4 + i, pl.ds(g * SUB, SUB), :] = done[i][g]
        put(q).start()
        return sums

    begin = [[content[pl.ds(y * members + g * SUB, SUB), :] for g in range(groups)] for y in edge_rows]
    middle_level = levels // 2
    sums = lax.fori_loop(0, middle_level // 2, functools.partial(two_levels, part_a, coef_a, 0), begin, unroll=2)
    sums = lax.fori_loop(middle_level // 2, levels // 2,
                         functools.partial(two_levels, part_b, coef_b, middle_level), sums, unroll=2)
    for y, row in zip(edge_rows, sums):
        for g in range(groups):
            content[pl.ds(y * members + g * SUB, SUB), :] = row[g]
    content16[...] = (content[...] / math.sqrt(levels)).astype(BF16)
    rays[...] = jnp.zeros_like(rays)
    live = count[0]
    mine = lax.axis_index("lat")
    for k in range(slots):
        picked = content16[pl.ds(pl.multiple_of(row_of[k] * members, members), members), :]
        partial = jnp.dot(picked, pw[k], preferred_element_type=F32)
        partial = jnp.where(k < live, partial, 0.0)
        place = block_of[k] - mine * blocks_dev
        place = jnp.where(place < 0, place + lat_size * blocks_dev, place)
        at = pl.ds(pl.multiple_of(place * members, members), members)
        rays[at, :] += partial
    size = blocks_dev * members
    for s in range(lat_size):
        outs[s][...] = rays[pl.ds(s * size, size), :]
    for q in range(levels // 2):
        put(q).wait()


def boundary(dims, state, inside, sides, corner_s, corner_n, below, above, block_of, row_of, count, lat_size, blocks_dev):
    members, levels, rows, width = dims
    slots, _, block = inside[3].shape
    size = blocks_dev * members
    return pl.pallas_call(
        functools.partial(boundary_kernel, dims, lat_size, slots, blocks_dev),
        name="boundary_rays",
        out_shape=[pltpu.HBM((levels * 4, members, width), F32), VMEM((2 * members, width), F32)]
        + [VMEM((size, block), F32)] * lat_size,
        in_specs=[IN_SMEM] * 3 + [IN_VMEM] * 15,
        out_specs=[IN_HBM] + [IN_VMEM] * (1 + lat_size),
        scratch_shapes=[
            VMEM((rows * members, width), F32),
            VMEM((rows * members, width), BF16),
            VMEM((lat_size * size, block), F32),
            VMEM((levels * 4, members, width), F32),
            pltpu.SemaphoreType.DMA((levels // 2,)),
        ],
        **grant(8, 30_000_000, 12_000_000),
    )(block_of, row_of, count, *near(state, *inside, *sides, corner_s, corner_n, below, above))


def spread_kernel(dims, inner_a, inner_b, fix, fix_ends, outer_hbm, hi_hbm, lo_hbm, centre_ref,
                  outer, hi_ref, lo_ref, outer_sem, hi_sem, lo_sem):
    members, levels, rows, width = dims
    sub = subs_of((rows, width))
    lane = lanes_of((members, width))
    near_edge = (lane < 2) | (lane >= width - 2)
    edge_rows = {0: 0, 1: 1, rows - 2: 2, rows - 1: 3}

    def get(q):
        part = pl.ds(q * 8, 8)
        return pltpu.make_async_copy(outer_hbm.at[part], outer.at[part], outer_sem.at[q])

    def put_hi(q):
        return pltpu.make_async_copy(hi_ref.at[q], hi_hbm.at[q], hi_sem.at[q])

    def put_lo(q):
        return pltpu.make_async_copy(lo_ref.at[q], lo_hbm.at[q], lo_sem.at[q])

    def begin(q, carry):
        get(q).start()
        return carry

    def pair(inner, offset, q, carry):
        get(q).wait()
        for h in range(2):
            l = q * 2 + h
            turn = (width - (width // levels) * l) % width
            mean = jnp.zeros((rows, width), F32)
            for y in range(rows):
                v = outer[l * 4 + edge_rows[y]] if y in edge_rows else inner[(l - offset) * (rows - 4) + y - 2]
                if y in (0, rows - 1):
                    add = fix_ends[pl.ds((0 if y == 0 else 1) * members, members), :]
                else:
                    add = fix[pl.ds(y * members, members), :]
                v = v + jnp.where(near_edge, pltpu.roll(add, turn, 1), 0.0)
                m = jnp.sum(v, axis=0, keepdims=True) / members
                mean = jnp.where(sub == y, m, mean)
                a = v - m
                hi = a.astype(BF16)
                to = (q, pl.ds(y * members, members), pl.ds(h * width, width))
                hi_ref[to] = hi
                lo_ref[to] = (a - hi.astype(F32)).astype(BF16)
            centre_ref[pl.ds(pl.multiple_of(l * rows, rows), rows), :] = mean
        put_hi(q).start()
        put_lo(q).start()
        return carry

    def finish(q, carry):
        put_hi(q).wait()
        put_lo(q).wait()
        return carry

    lax.fori_loop(0, levels // 2, begin, 0)
    lax.fori_loop(0, levels // 4, functools.partial(pair, inner_a, 0), 0)
    lax.fori_loop(levels // 4, levels // 2, functools.partial(pair, inner_b, levels // 2), 0)
    lax.fori_loop(0, levels // 2, finish, 0)


def anomalies(dims, inners, outer, fix, fix_ends):
    members, levels, rows, width = dims
    shape = (levels // 2, rows * members, 2 * width)
    return pl.pallas_call(
        functools.partial(spread_kernel, dims),
        name="anomalies",
        out_shape=(pltpu.HBM(shape, BF16), pltpu.HBM(shape, BF16), VMEM((levels * rows, width), F32)),
        in_specs=[IN_VMEM] * 4 + [IN_HBM],
        out_specs=[IN_HBM] * 2 + [IN_VMEM],
        scratch_shapes=[VMEM(outer.shape, F32), VMEM(shape, BF16), VMEM(shape, BF16)]
        + [pltpu.SemaphoreType.DMA((levels // 2,))] * 3,
        **grant(12, 8_000_000, 8_000_000),
    )(*near(*inners, fix, fix_ends), *far(outer))


def moments_kernel(members, blocks_dev, block, n_parts, devices, *refs):
    parts, (obs_ref, var_ref, prior_ref, innov_ref, packed_ref) = refs[:n_parts], refs[n_parts:]
    scaled, both = [], []
    for b in range(blocks_dev):
        at = pl.ds(b * members, members)
        total = parts[0][at, :]
        for part in parts[1:]:
            total = total + part[at, :]
        prior_ref[:, pl.ds(b * block, block)] = total
        mean = jnp.sum(total, axis=0, keepdims=True) / members
        dev = total - mean
        var = var_ref[pl.ds(b, 1), :]
        misfit = obs_ref[pl.ds(b, 1), :] - mean
        innov_ref[pl.ds(b, 1), :] = misfit / jnp.sqrt(var)
        scaled.append(dev / var)
        both.append(jnp.concatenate([dev, jnp.broadcast_to(misfit, (SUB, block))], axis=0))
    left = jnp.concatenate(scaled, axis=1)
    right = jnp.concatenate(both, axis=1)
    g = lax.dot_general(left, right, (((1,), (1,)), ((), ())), precision=lax.Precision.HIGHEST,
                        preferred_element_type=F32)
    wide = jnp.concatenate([g, jnp.zeros((members, 128 - g.shape[1]), F32)], axis=1)
    lane = lanes_of((SUB, 128))
    packed = jnp.zeros((SUB, 128), F32)
    groups = members // SUB
    start = 0
    for i in range(groups):
        v = wide[i * SUB:(i + 1) * SUB]
        stop = start + SUB * (i + 1)
        moved = pltpu.roll(v, start, 1) if start else v
        packed = jnp.where((lane >= start) & (lane < stop), moved, packed)
        start = stop
    for i in range(groups):
        v = wide[i * SUB:(i + 1) * SUB]
        packed = jnp.where(lane == start + i, pltpu.roll(v, start + i - members, 1), packed)
    for device in range(devices):
        packed_ref[pl.ds(device * SUB, SUB), :] = packed


def moments(parts, obs, var, members, blocks_dev, block, devices):
    return pl.pallas_call(
        functools.partial(moments_kernel, members, blocks_dev, block, len(parts), devices),
        name="moments",
        out_shape=(jax.ShapeDtypeStruct((members, blocks_dev * block), F32),
                   jax.ShapeDtypeStruct((blocks_dev, block), F32),
                   VMEM((devices * SUB, 128), F32)),
        in_specs=[IN_VMEM] * (len(parts) + 2),
        out_specs=[IN_VMEM] * 3,
        **grant(8, 4_000_000, 400_000),
    )(*near(*parts), obs, var)


def weights(gathered, members, devices):
    groups = members // SUB
    lane = lanes_of((SUB, 128))
    sub = subs_of((SUB, 128))
    total = gathered[pl.ds(0, SUB), :]
    for d in range(1, devices):
        total = total + gathered[pl.ds(d * SUB, SUB), :]
    lower, start = [], 0
    for i in range(groups):
        v = pltpu.roll(total, (128 - start) % 128, 1) if start else total
        lower.append(jnp.where(lane < SUB * (i + 1), v, 0.0))
        start += SUB * (i + 1)
    upper = jnp.transpose(jnp.concatenate(lower, axis=0))
    upper = upper[:members]
    upper = jnp.concatenate([upper, jnp.zeros((members, 128 - members), F32)], axis=1)
    rows = []
    for i in range(groups):
        a = jnp.where(lane < SUB * (i + 1), lower[i], upper[i * SUB:(i + 1) * SUB])
        a = jnp.where(lane < members, a, 0.0)
        a = a + jnp.where(lane == sub + SUB * i, members - 1.0, 0.0)
        a = jnp.where(lane == members + sub + SUB * i, 1.0, a)
        pull = pltpu.roll(total, (2 * members - start - i) % 128, 1)
        rows.append(jnp.where(lane == 2 * members, pull, a))
    for k in range(0, members, 2):
        i0, s = divmod(k, SUB)
        f0 = [jnp.broadcast_to(r[:, k:k + 1], (SUB, 128)) for r in rows]
        f1 = [jnp.broadcast_to(r[:, k + 1:k + 2], (SUB, 128)) for r in rows]
        row0, row1 = spread(rows[i0], s), spread(rows[i0], s + 1)
        a, b, d = spread(f0[i0], s), spread(f1[i0], s), spread(f1[i0], s + 1)
        inv = 1.0 / a
        slope = b * inv
        low = row1 - slope * row0
        ratio0 = row0 * inv
        ratio1 = low * (1.0 / (d - slope * b))
        for i in range(i0, groups):
            g1 = f1[i] - slope * f0[i]
            change = f0[i] * ratio0
            second = g1 * ratio1
            if i == i0:
                change = jnp.where(sub > s, change, 0.0)
                second = jnp.where(sub > s + 1, second, 0.0)
            rows[i] = rows[i] - change - second
    mean_weight = jnp.zeros((SUB, 128), F32)
    for i in range(groups):
        pivot = jnp.sum(jnp.where(lane == sub + SUB * i, rows[i], 0.0), axis=1, keepdims=True)
        rows[i] = rows[i] / jnp.sqrt(pivot)
        mean_weight = mean_weight + rows[i] * rows[i][:, 2 * members:2 * members + 1]
    mean_weight = jnp.sum(mean_weight, axis=0, keepdims=True)
    return [mean_weight + math.sqrt(members - 1.0) * r for r in rows]


def update_kernel(dims, devices, gathered, centre_ref, hi_hbm, lo_hbm, out_hbm, mat_hi, mat_lo, done, hi_ref, lo_ref, sem, part_sem):
    members, levels, rows, width = dims
    half = levels // 4

    def get(source, target, part, k):
        at = pl.ds(part * half, half)
        return pltpu.make_async_copy(source.at[at], target.at[at], part_sem.at[k, part])

    for part in range(2):
        get(hi_hbm, hi_ref, part, 0).start()
        get(lo_hbm, lo_ref, part, 1).start()
    size = rows * members
    lane = lanes_of((rows, 128))
    sub = subs_of((rows, 128))
    copies = 128 // members
    made = weights(gathered, members, devices)
    for i, r in enumerate(made):
        r = jnp.where(lane < members, pltpu.roll(r, 128 - members, 1), 0.0)
        tiled = r
        for q in range(1, copies):
            tiled = tiled + pltpu.roll(r, q * members, 1)
        for s in range(0, SUB, 2):
            b = i * SUB + s
            for h in range(size // 128):
                keep = (lane // members) + h * copies == sub
                two = [jnp.where(keep, jnp.broadcast_to(tiled[t:t + 1], (rows, 128)), 0.0) for t in (s, s + 1)]
                m = jnp.concatenate(two, axis=0)
                big = m.astype(BF16)
                to = (pl.ds(b * rows, 2 * rows), pl.ds(h * 128, 128))
                mat_hi[to] = big
                mat_lo[to] = (m - big.astype(F32)).astype(BF16)

    def copy(q):
        part = pl.ds(q * 2, 2)
        return pltpu.make_async_copy(done.at[:, part], out_hbm.at[:, part], sem.at[q])

    def pair(q, carry):
        dot = functools.partial(jnp.dot, preferred_element_type=F32)
        hi = hi_ref[q]
        acc = dot(mat_hi[...], hi) + dot(mat_hi[...], lo_ref[q]) + dot(mat_lo[...], hi)
        for h in range(2):
            l = q * 2 + h
            centre = centre_ref[pl.ds(pl.multiple_of(l * rows, rows), rows), :]
            done[:, l] = acc[:, h * width:(h + 1) * width].reshape(members, rows, width) + centre[None]
        copy(q).start()
        return carry

    for part in range(2):
        get(hi_hbm, hi_ref, part, 0).wait()
        get(lo_hbm, lo_ref, part, 1).wait()
        lax.fori_loop(part * half, (part + 1) * half, pair, 0, unroll=8)

    def finish(q, carry):
        copy(q).wait()
        return carry

    lax.fori_loop(0, levels // 2, finish, 0)


def update(gathered, hi, lo, centre, dims, devices):
    members, levels, rows, _ = dims
    return pl.pallas_call(
        functools.partial(update_kernel, dims, devices),
        name="update",
        out_shape=jax.ShapeDtypeStruct(dims, F32),
        in_specs=[IN_VMEM] * 2 + [IN_HBM] * 2,
        out_specs=IN_HBM,
        scratch_shapes=[VMEM((rows * members, rows * members), BF16)] * 2
        + [VMEM(dims, F32), VMEM(lo.shape, BF16), VMEM(lo.shape, BF16), pltpu.SemaphoreType.DMA((levels // 2,)),
           pltpu.SemaphoreType.DMA((2, 2))],
        **grant(14, 2_000_000_000, 8_000_000),
    )(*near(gathered, centre), *far(hi, lo))


def per_device(sample_deviations, east_courant, north_courant, production, loss_rate, entry_count, entry_row,
               entry_block, path_weight, observed, obs_var):
    dims = members, levels, rows, width = sample_deviations.shape
    lat_size, lon_size = lax.axis_size("lat"), lax.axis_size("lon")
    block = path_weight.shape[2]
    blocks_dev = observed.shape[0] // block
    ring = lambda n, s: [(i, (i + s) % n) for i in range(n)]
    up = [(i, i + 1) for i in range(lat_size - 1)]
    down = [(j, i) for i, j in up]

    fields = (east_courant, north_courant, production, loss_rate)
    state, to_north, to_south, edge, to_east, to_west, local = pack(sample_deviations, fields)
    west = lax.ppermute(to_east, "lon", ring(lon_size, 1))
    east = lax.ppermute(to_west, "lon", ring(lon_size, lon_size - 1))
    below = lax.ppermute(to_north, "lat", up)
    above = lax.ppermute(to_south, "lat", down)
    half = levels // 2
    inner_a, *inside_a = interior(dims, 0, half, state, local, path_weight)
    first, last = corners(dims, edge, west, east)
    corner_s = lax.ppermute(last, "lat", up)
    corner_n = lax.ppermute(first, "lat", down)
    inner_b, *inside_b = interior(dims, half, levels - half, state, local)
    sides = columns(dims, edge, west, east)
    outer, fix_ends, *sums = boundary(dims, state, inside_a + inside_b, sides, corner_s, corner_n, below, above,
                            entry_block, entry_row, entry_count, lat_size, blocks_dev)
    got = [sums[0]] + [lax.ppermute(sums[s], "lat", ring(lat_size, s)) for s in range(1, lat_size)]
    hi, lo, centre = anomalies(dims, (inner_a, inner_b), outer, sides[0], fix_ends)
    devices = lat_size * lon_size
    prior, innovation, packed = moments(got, observed.reshape(blocks_dev, block), obs_var.reshape(blocks_dev, block),
                                        members, blocks_dev, block, devices)
    gathered = lax.all_to_all(packed, ("lon", "lat"), 0, 0, tiled=True)
    updated = update(gathered, hi, lo, centre, dims, devices)
    return updated, prior, innovation.reshape(observed.shape)


def solution(mesh):
    tile = P(None, "lat", "lon")
    owned = P(("lon", "lat"))
    in_specs = (P(None, None, "lat", "lon"), tile, tile, tile, tile, owned, owned, owned,
                P(("lon", "lat"), None, None), owned, owned)
    out_specs = (P(None, None, "lat", "lon"), P(None, ("lon", "lat")), owned)
    return jax.shard_map(per_device, mesh=mesh, in_specs=in_specs, out_specs=out_specs, check_vma=False)
```
